32 devices in a mesh: elem: 16 (over z, x, core), mode: 2 (over y).
Axes of the slice: x: 2, y: 2, z: 4, core: 2. Of those that a mesh axis runs over, the one named last changes fastest.
Arguments:
- velocity: float32 [1024, 128, 128], P(None, ('elem', 'mode')), may hold values from -6 to 6
- previous: float32 [1024, 128, 128], P('mode', 'elem'), may hold values from -6 to 6
- derivative: float32 [128, 128], replicated, may hold values from -0.5 to 0.5
- stiffness: float32 [128, 128], replicated, as said below
- coupling: float32 [4, 128, 128], replicated, may hold values from -0.25 to 0.25
- reaction: float32 [128], P('elem'), may hold values from 0.5 to 4
- axial_weight: float32 [128], P('elem'), may hold values from 0.5 to 4
- neighbours: int32 [128, 4], P('elem'), may hold values from -1 to 127, as said below
Outputs:
- solution: float32 [1024, 128, 128], P('mode', 'elem')
The draws below stay inside these ranges and needn't reach their ends.
Inputs may be any that keep to these rules, and one draw needn't show every extreme that they name: `stiffness`: symmetric with a positive diagonal. `neighbours`: elements lie on a grid of 2 rows, periodic along the rows, and 4 columns a group of 8 elements, groups in order along the columns with walls at both ends. A group's first 2 elements form its first column and its last 2 its last column; a neighbour in another group is in the next or previous group, among its first or last 2 elements.
All inputs are finite; a program needn't handle non-finite values.
Results may differ from the reference program's by a relative error of at most 0.0001.
Values sent between devices are 32-bit elements; how exact they have to be, the bound alone decides.
A program may use at most 128 MiB of HBM per device.

```python
import math
import jax
import jax.numpy as jnp
from jax import lax

Q = 128
NZ = 1024
EG = 8
EY = 2
E = 128


def draw_stiffness(key, part):
    first_key, second_key = jax.random.split(jax.random.fold_in(key, 11))
    diagonal = jax.random.uniform(first_key, (Q,), jnp.float32, 2.0, 6.0)
    noise = jax.random.normal(second_key, (Q, Q), jnp.float32) * (0.3 / math.sqrt(Q))
    return jnp.diag(diagonal) + 0.5 * (noise + noise.T)


def draw_neighbours(key, part):
    groups = E // EG
    columns = EG // EY
    places = jnp.arange(EG, dtype=jnp.int32)
    column_of = places // EY
    column_kind = jnp.where(column_of == 0, 0, jnp.where(column_of == columns - 1, 2, 1)).astype(jnp.int32)

    def arrange(group_index):
        shuffle = jax.random.permutation(jax.random.fold_in(jax.random.fold_in(key, 23), group_index), EG).astype(jnp.int32)
        slot_place = jnp.argsort(column_kind * EG + shuffle, stable=True).astype(jnp.int32)
        place_slot = jnp.argsort(slot_place, stable=True).astype(jnp.int32)
        return (slot_place, place_slot)
    orders, slots = jax.vmap(arrange)(jnp.arange(groups, dtype=jnp.int32))
    element_place = orders.reshape(-1)
    group_of = jnp.arange(E, dtype=jnp.int32) // EG
    grid_col = group_of * columns + element_place // EY
    grid_row = element_place % EY
    total_cols = groups * columns

    def element_at(column_at, row_at):
        group_at = column_at // columns
        place_at = column_at % columns * EY + row_at
        return group_at * EG + slots[group_at, place_at]
    left_id = jnp.where(grid_col > 0, element_at(jnp.maximum(grid_col - 1, 0), grid_row), -1)
    right_id = jnp.where(grid_col < total_cols - 1, element_at(jnp.minimum(grid_col + 1, total_cols - 1), grid_row), -1)
    down_id = element_at(grid_col, (grid_row + EY - 1) % EY)
    up_id = element_at(grid_col, (grid_row + 1) % EY)
    return jnp.stack([left_id, right_id, down_id, up_id], axis=1).astype(jnp.int32)


def block_scale(key, dims, cuts, smallest, top_value):
    gain, own = 1.0, jax.random.fold_in(key, 6)
    for dim, parts in cuts:
        heights = jnp.exp(jax.random.uniform(jax.random.fold_in(own, dim), (parts,), jnp.float32, smallest / len(cuts), top_value / len(cuts)))
        gain = gain * jnp.repeat(heights, dims[dim] // parts).reshape([-1 if axis == dim else 1 for axis in range(len(dims))])
    return gain


def normal_values(rng, extent, width, most, cuts=(), kind=jnp.bfloat16):
    array = jax.random.normal(rng, extent, jnp.float32) * width
    if len(cuts) > 0:
        array = block_scale(rng, extent, cuts, -0.22, 0.18) * array
    return jnp.clip(array, min=-most, max=most).astype(kind)


def setup_inputs(seed: int = 0) -> dict:
    key_of = jax.random.split(jax.random.key(seed), 9)
    velocity = normal_values(key_of[0], (NZ, E, Q), 1.0, 6.0, ((1, 32),), jnp.float32)
    previous = normal_values(key_of[1], (NZ, E, Q), 1.0, 6.0, ((0, 2), (1, 16)), jnp.float32)
    derivative = normal_values(key_of[2], (Q, Q), Q ** -0.5, 0.5, (), jnp.float32)
    stiffness = draw_stiffness(jax.random.fold_in(key_of[8], 71), 0)
    coupling = normal_values(key_of[4], (4, Q, Q), (4 * Q) ** -0.5, 0.25, (), jnp.float32)
    reaction = jnp.clip(jnp.exp(math.log(4.0) - 2.0794415 * jax.random.uniform(key_of[5], (E,), jnp.float32) ** block_scale(key_of[5], (E,), ((0, 16),), -0.2, 0.2)), 0.5, 4.0)
    axial_weight = jnp.clip(jnp.exp(math.log(4.0) - 2.0794415 * jax.random.uniform(key_of[6], (E,), jnp.float32) ** block_scale(key_of[6], (E,), ((0, 16),), -0.2, 0.2)), 0.5, 4.0)
    neighbours = draw_neighbours(jax.random.fold_in(key_of[8], 71), 0)
    return dict(velocity=velocity, previous=previous, derivative=derivative, stiffness=stiffness, coupling=coupling, reaction=reaction, axial_weight=axial_weight, neighbours=neighbours)


highest = lax.Precision.HIGHEST
dt_step = 0.5
first_weight = 0.7
second_weight = 1.1


def row_shift(count):
    rows = jnp.arange(count, dtype=jnp.int32)
    half = count // 2
    waves = jnp.where(rows <= half, rows, rows - half).astype(jnp.float32)
    return 4.0 * (waves / half) ** 2


def reference(velocity, previous, derivative, stiffness, coupling, reaction, axial_weight, neighbours):
    slope = jnp.einsum('zeq,pq->zep', velocity, derivative, precision=highest)
    product = velocity - dt_step * velocity * slope
    spectrum = jnp.fft.rfft(product, axis=0)
    half = NZ // 2
    rhs = jnp.concatenate([spectrum.real[:half], spectrum.real[half:half + 1], spectrum.imag[1:half]], axis=0) * (NZ ** -0.5)
    shifts = row_shift(NZ).astype(rhs.dtype)
    present = neighbours >= 0
    near_index = jnp.where(present, neighbours, 0).astype(jnp.int32)
    face_mask = present.astype(rhs.dtype)
    stiff_diag = jnp.diagonal(stiffness)

    def apply(field, shift_rows):
        result = jnp.einsum('req,pq->rep', field, stiffness, precision=highest)
        result = result + (reaction[None, :, None] + shift_rows[:, None, None] * axial_weight[None, :, None]) * field
        for side_index in range(4):
            beside = jnp.take(field, near_index[:, side_index], axis=1) * face_mask[None, :, side_index, None]
            result = result + jnp.einsum('req,pq->rep', beside, coupling[side_index], precision=highest)
        return result

    def sweep_block(inputs):
        rhs_rows, start_rows, shift_rows = inputs
        inverse = 1.0 / (stiff_diag[None, None, :] + reaction[None, :, None] + shift_rows[:, None, None] * axial_weight[None, :, None])
        first = start_rows + first_weight * inverse * (rhs_rows - apply(start_rows, shift_rows))
        return first + second_weight * inverse * (rhs_rows - apply(first, shift_rows))

    blocks = 16
    rows_block = NZ // blocks
    result = lax.map(sweep_block, (rhs.reshape(blocks, rows_block, E, Q), previous.reshape(blocks, rows_block, E, Q), shifts.reshape(blocks, rows_block)))
    return result.reshape(NZ, E, Q)
```

```python
import functools
import math

import jax
import jax.numpy as jnp
import ml_dtypes
import numpy as np
from jax import lax
from jax.experimental import pallas as pl
from jax.experimental.pallas import tpu as pltpu
from jax.sharding import PartitionSpec as P

dt_step = 0.5
first_weight = 0.7
second_weight = 1.1
CHUNKS = 8
vmem_bytes = 67043328
vmem_spare = 262144
MESH = pl.DeviceIdType.MESH
bf16 = jnp.bfloat16
f32 = jnp.float32


def dft_tables(planes, modes):
    half = planes // 2
    rows = np.arange(planes)
    waves = np.where(rows <= half, rows, rows - half)
    phase = (waves[:, None] * np.arange(half)[None, :]) % planes
    angles = 2.0 * math.pi / planes * phase
    table = np.where((rows <= half)[:, None], np.cos(angles), -np.sin(angles)) * planes ** (-0.5)
    table = table.reshape(modes, planes // modes // 2, 2, half).transpose(0, 2, 1, 3)
    high = table.astype(ml_dtypes.bfloat16)
    low = (table - high.astype(np.float64)).astype(ml_dtypes.bfloat16)
    return np.stack([high, low], axis=2)


def split(values):
    high = values.astype(bf16)
    low = (values - high.astype(f32)).astype(bf16)
    return high, low


def kernel(
    modes, groups, planes, elems, group_elems, rows, nodes,
    vel_hbm, prev_hbm, table_hbm, der_hbm, stiff_hbm, coup_hbm, reac, axial, near,
    outv,
    vel, prev, table, der, stiff, coup, w_slope, w_apply, folded, sent, rhs, first, inverse,
    halo_prev, halo_first, pairs,
    vel_sem, table_sem, prev_sem, small_sem, y_send, y_recv, p_send, p_recv, f_send, f_recv,
):
    half = planes // 2
    rim = group_elems // 4
    count = rows // CHUNKS
    per_parity = CHUNKS // 2
    early = min(rim, elems)
    spans = [(0, early)] + ([(early, elems)] if early < elems else [])
    faces = faces_of(group_elems)
    me = lax.axis_index("mode")
    group = lax.axis_index("elem")
    zero_slot = group_elems + 2 * rim

    def skip(mode):
        return jnp.where(mode < modes // 2, 0, elems - early)

    def element_of(mode, slot):
        if isinstance(mode, int):
            turn = 0 if mode < modes // 2 else elems - early
            return mode * elems + (slot + turn) % elems
        return mode * elems + lax.rem(slot + skip(mode), elems)

    def slot_of(element):
        mode, place = element // elems, element % elems
        turn = 0 if mode < modes // 2 else elems - early
        return mode, (place - turn) % elems

    barrier = pltpu.get_barrier_semaphore()
    for step in range(1, modes):
        pl.semaphore_signal(
            barrier, inc=1, device_id={"mode": lax.rem(me + step, modes)}, device_id_type=MESH
        )
    has_left = group > 0
    has_right = group < groups - 1

    @pl.when(has_left)
    def _():
        pl.semaphore_signal(barrier, inc=1, device_id={"elem": group - 1}, device_id_type=MESH)

    @pl.when(has_right)
    def _():
        pl.semaphore_signal(barrier, inc=1, device_id={"elem": group + 1}, device_id_type=MESH)

    der_load = pltpu.make_async_copy(der_hbm, der, small_sem.at[0])
    stiff_load = pltpu.make_async_copy(stiff_hbm, stiff, small_sem.at[1])
    coup_load = pltpu.make_async_copy(coup_hbm, coup, small_sem.at[2])

    def vel_load(slot):
        return pltpu.make_async_copy(
            vel_hbm.at[:, lax.rem(slot + skip(me), elems)], vel.at[slot], vel_sem.at[slot]
        )

    def table_load(step, parity):
        owner = lax.rem(me + step, modes)
        return pltpu.make_async_copy(
            table_hbm.at[owner, parity], table.at[step, parity], table_sem.at[step, parity]
        )

    def prev_load(parity, e):
        return pltpu.make_async_copy(
            prev_hbm.at[:, parity, e], prev.at[parity, e], prev_sem.at[parity, e]
        )

    steps = [*range(1, modes), 0]
    der_load.start()
    for slot in range(early):
        vel_load(slot).start()
    for parity in range(2):
        for step in range(1, modes):
            table_load(step, parity).start()
    for slot in range(early, elems):
        vel_load(slot).start()
    for parity in range(2):
        table_load(0, parity).start()
    for parity in range(2):
        for e in range(group_elems):
            prev_load(parity, e).start()
    stiff_load.start()
    coup_load.start()

    def halo_copies(source, halo, send, recv, c):
        right = pltpu.make_async_remote_copy(
            source(c, 0), halo.at[0, c], send.at[0, c], recv.at[0, c],
            device_id={"elem": group + 1}, device_id_type=MESH,
        )
        left = pltpu.make_async_remote_copy(
            source(c, 1), halo.at[1, c], send.at[1, c], recv.at[1, c],
            device_id={"elem": group - 1}, device_id_type=MESH,
        )
        return right, left

    def prev_rim(c, side, i):
        parity, place = c // per_parity, c % per_parity
        return pltpu.make_async_remote_copy(
            prev_hbm.at[
                pl.ds(place * count, count), parity, (group_elems - rim) * (1 - side) + i
            ],
            halo_prev.at[side, c, i], p_send.at[side, c, i], p_recv.at[side, c, i],
            device_id={"elem": group + 1 - 2 * side}, device_id_type=MESH,
        )

    def first_copies(c):
        def source(c, side):
            return first.at[c, pl.ds((group_elems - rim) * (1 - side), rim)]

        return halo_copies(source, halo_first, f_send, f_recv, c)

    def start_halo(copies):
        right, left = copies
        pl.when(has_right)(right.start)
        pl.when(has_left)(left.start)

    def wait_halo_recv(copies):
        right, left = copies
        pl.when(has_left)(right.wait_recv)
        pl.when(has_right)(left.wait_recv)

    def wait_halo_send(copies):
        right, left = copies
        pl.when(has_right)(right.wait_send)
        pl.when(has_left)(left.wait_send)

    def each_prev_rim(c, side, act):
        for i in range(rim):
            act(prev_rim(c, side, i))

    pl.semaphore_wait(
        barrier, modes - 1 + has_left.astype(jnp.int32) + has_right.astype(jnp.int32)
    )

    def send_prev(c, carry):
        pl.when(has_right)(lambda: each_prev_rim(c, 0, lambda copy: copy.start()))
        pl.when(has_left)(lambda: each_prev_rim(c, 1, lambda copy: copy.start()))
        return carry

    lax.fori_loop(0, CHUNKS, send_prev, 0)

    def set_weights(ref, at, matrix):
        high, low = split(matrix.T)
        for part in range(2):
            ref[pl.ds(at + part * nodes, nodes), pl.ds(0, nodes)] = high
            ref[pl.ds(at + part * nodes, nodes), pl.ds(nodes, nodes)] = low

    der_load.wait()
    set_weights(w_slope, 0, der[...])

    block = min(256, half)

    def advect(slot):
        vel_load(slot).wait()
        for b in range(half // block):
            lower = vel[slot, pl.ds(b * block, block), :]
            upper = vel[slot, pl.ds(half + b * block, block), :]
            values = jnp.concatenate([lower, upper], axis=0)
            both = jnp.dot(
                jnp.concatenate(split(values), axis=1), w_slope[...], preferred_element_type=f32
            )
            slope = both[:, :nodes] + both[:, nodes:]
            product = values - dt_step * values * slope
            lower, upper = product[:block], product[block:]
            for parity, value in enumerate((lower + upper, lower - upper)):
                high, low = split(value)
                where = (pl.ds(b * block, block), pl.ds(slot * nodes, nodes))
                folded[(parity, 0) + where] = high
                folded[(parity, 1) + where] = low

    def transform(step, parity, start, stop):
        span = pl.ds(start * nodes, (stop - start) * nodes)
        data_high, data_low = folded[parity, 0, :, span], folded[parity, 1, :, span]
        t_high, t_low = table[step, parity, 0], table[step, parity, 1]
        return (
            jnp.dot(t_high, data_high, preferred_element_type=f32)
            + jnp.dot(t_low, data_high, preferred_element_type=f32)
            + jnp.dot(t_high, data_low, preferred_element_type=f32)
        )

    def put_rows(ref, parity, block_rows, start, stop):
        for j in range(per_parity):
            for slot in range(start, stop):
                at = (slot - start) * nodes
                ref[parity * per_parity + j, slot] = block_rows[
                    j * count : (j + 1) * count, at : at + nodes
                ]

    def y_copy(step, c, k):
        start, stop = spans[k]
        return pltpu.make_async_remote_copy(
            sent.at[step - 1, c, pl.ds(start, stop - start)],
            rhs.at[me, c, pl.ds(start, stop - start)],
            y_send.at[k, step - 1, c], y_recv.at[k, step - 1, c],
            device_id={"mode": lax.rem(me + step, modes)}, device_id_type=MESH,
        )

    for k, (start, stop) in enumerate(spans):
        for slot in range(start, stop):
            advect(slot)
        for parity in range(2):
            for step in range(1, modes):
                if k == 0:
                    table_load(step, parity).wait()
                put_rows(sent.at[step - 1], parity, transform(step, parity, start, stop), start, stop)
                for j in range(per_parity):
                    y_copy(step, parity * per_parity + j, k).start()

    for parity in range(2):
        table_load(0, parity).wait()
        put_rows(rhs.at[me], parity, transform(0, parity, 0, elems), 0, elems)

    stiff_load.wait()
    coup_load.wait()
    set_weights(w_apply, 0, stiff[...])
    for f in range(faces):
        matrix = coup[f] + coup[f + 1] if f == faces - 1 and faces < 4 else coup[f]
        set_weights(w_apply, 2 * nodes * (f + 1), matrix)
    eye = lax.broadcasted_iota(jnp.int32, (nodes, nodes), 0) == lax.broadcasted_iota(
        jnp.int32, (nodes, nodes), 1
    )
    diagonal = jnp.sum(jnp.where(eye, stiff[...], 0.0), axis=0, keepdims=True)
    pairs[zero_slot] = jnp.zeros((count, 2 * nodes), bf16)
    for parity in range(2):
        for e in range(group_elems):
            prev_load(parity, e).wait()

    def put_pair(slot, value):
        high, low = split(value)
        pairs[slot, :, pl.ds(0, nodes)] = high
        pairs[slot, :, pl.ds(nodes, nodes)] = low

    def put_halo(halo, c):
        @pl.when(has_left)
        def _():
            for i in range(rim):
                put_pair(i, halo[0, c, i])

        @pl.when(has_right)
        def _():
            for i in range(rim):
                put_pair(rim + group_elems + i, halo[1, c, i])

    def apply():
        columns = [
            jnp.concatenate([pairs[rim + e] for e in range(group_elems)], axis=0)
        ]
        for f in range(faces):
            found = []
            for e in range(group_elems):
                n = near[f, e]
                slot = jnp.clip(n - group * group_elems + rim, 0, zero_slot - 1)
                slot = jnp.where(n >= 0, slot, zero_slot)
                found.append(pairs[slot])
            columns.append(jnp.concatenate(found, axis=0))
        both = jnp.dot(
            jnp.concatenate(columns, axis=1), w_apply[...], preferred_element_type=f32
        )
        return both[:, :nodes] + both[:, nodes:]

    def prev_rows(c, e):
        return prev[c // per_parity, e, pl.ds((c % per_parity) * count, count), :]

    def shifts(c):
        places = lax.broadcasted_iota(jnp.int32, (count, nodes), 0)
        row = me * rows + 2 * ((c % per_parity) * count + places) + c // per_parity
        wave = jnp.where(row <= half, row, row - half).astype(f32)
        return 4.0 * (wave / half) ** 2

    def complete(c, mode, slot, e):
        first[c, e] = first[c, e] + first_weight * inverse[c, e] * rhs[mode, c, slot]

    def first_sweep(c, carry):
        for e in range(group_elems):
            put_pair(rim + e, prev_rows(c, e))
        pl.when(has_left)(lambda: each_prev_rim(c, 0, lambda copy: copy.wait_recv()))
        pl.when(has_right)(lambda: each_prev_rim(c, 1, lambda copy: copy.wait_recv()))
        put_halo(halo_prev, c)
        applied = apply()
        shift = shifts(c)
        for e in range(group_elems):
            scaling = reac[e] + shift * axial[e]
            recip = 1.0 / (diagonal + scaling)
            inverse[c, e] = recip
            value = prev_rows(c, e)
            part = applied[e * count : (e + 1) * count]
            first[c, e] = value - first_weight * recip * (part + scaling * value)
        for slot in range(early, elems):
            complete(c, me, slot, element_of(me, slot))
        for step in range(1, modes):
            y_copy(step, c, 0).wait_recv()
        for mode in range(modes):
            for slot in range(early):
                complete(c, mode, slot, element_of(mode, slot))
        start_halo(first_copies(c))
        return carry

    def second_sweep(c, carry):
        for mode in range(modes):
            for slot in range(early):
                e = element_of(mode, slot)
                put_pair(rim + e, first[c, e])
        for slot in range(early, elems):
            e = element_of(me, slot)
            put_pair(rim + e, first[c, e])
        wait_halo_recv(first_copies(c))
        put_halo(halo_first, c)
        if early < elems:
            for step in range(1, modes):
                y_copy(step, c, 1).wait_recv()
                mode = lax.rem(me + step, modes)
                for slot in range(early, elems):
                    e = element_of(mode, slot)
                    complete(c, mode, slot, e)
                    put_pair(rim + e, first[c, e])
        applied = apply()
        shift = shifts(c)
        for e in range(group_elems):
            mode, slot = slot_of(e)
            scaling = reac[e] + shift * axial[e]
            value = first[c, e]
            part = applied[e * count : (e + 1) * count]
            start = (2 * (c % per_parity) * count + c // per_parity) * group_elems + e
            outv[pl.ds(start, count, stride=2 * group_elems), :] = value + second_weight * inverse[
                c, e
            ] * (rhs[mode, c, slot] - (part + scaling * value))
        return carry

    lax.fori_loop(0, CHUNKS, first_sweep, 0)
    lax.fori_loop(0, CHUNKS, second_sweep, 0)

    def finish(c, carry):
        pl.when(has_right)(lambda: each_prev_rim(c, 0, lambda copy: copy.wait_send()))
        pl.when(has_left)(lambda: each_prev_rim(c, 1, lambda copy: copy.wait_send()))
        wait_halo_send(first_copies(c))
        for k in range(len(spans)):
            for step in range(1, modes):
                y_copy(step, c, k).wait_send()
        return carry

    lax.fori_loop(0, CHUNKS, finish, 0)


def faces_of(group_elems):
    return 3 if group_elems // 4 == 2 else 4


def body(modes, groups, velocity, previous, derivative, stiffness, coupling, reaction, axial_weight, neighbours):
    planes, elems, nodes = velocity.shape
    rows, group_elems, _ = previous.shape
    half = planes // 2
    rim = group_elems // 4
    count = rows // CHUNKS
    tables = jnp.asarray(dft_tables(planes, modes))
    run = functools.partial(kernel, modes, groups, planes, elems, group_elems, rows, nodes)
    anywhere = pl.BlockSpec(memory_space=pltpu.HBM)
    scalar = pl.BlockSpec(memory_space=pltpu.SMEM)
    dma = pltpu.SemaphoreType.DMA
    taps = faces_of(group_elems) + 1
    scratch = [
        pltpu.VMEM((elems, planes, nodes), f32),
        pltpu.VMEM((2, group_elems, rows // 2, nodes), f32),
        pltpu.VMEM(tables.shape, bf16),
        pltpu.VMEM((nodes, nodes), f32),
        pltpu.VMEM((nodes, nodes), f32),
        pltpu.VMEM((4, nodes, nodes), f32),
        pltpu.VMEM((2 * nodes, 2 * nodes), bf16),
        pltpu.VMEM((taps * 2 * nodes, 2 * nodes), bf16),
        pltpu.VMEM((2, 2, half, elems * nodes), bf16),
        pltpu.VMEM((modes - 1, CHUNKS, elems, count, nodes), f32),
        pltpu.VMEM((modes, CHUNKS, elems, count, nodes), f32),
        pltpu.VMEM((CHUNKS, group_elems, count, nodes), f32),
        pltpu.VMEM((CHUNKS, group_elems, count, nodes), f32),
        pltpu.VMEM((2, CHUNKS, rim, count, nodes), f32),
        pltpu.VMEM((2, CHUNKS, rim, count, nodes), f32),
        pltpu.VMEM((group_elems + 2 * rim + 1, count, 2 * nodes), bf16),
    ]
    semaphores = [
        dma((elems,)),
        dma((modes, 2)),
        dma((2, group_elems)),
        dma((3,)),
        dma((2, modes - 1, CHUNKS)),
        dma((2, modes - 1, CHUNKS)),
        dma((2, CHUNKS, rim)),
        dma((2, CHUNKS, rim)),
        dma((2, CHUNKS)),
        dma((2, CHUNKS)),
    ]
    out = pl.pallas_call(
        run,
        out_shape=pltpu.VMEM((rows * group_elems, nodes), f32),
        in_specs=[anywhere] * 6 + [scalar] * 3,
        out_specs=pl.BlockSpec(memory_space=pltpu.VMEM),
        scratch_shapes=scratch + semaphores,
        compiler_params=pltpu.CompilerParams(
            collective_id=0, has_side_effects=True, vmem_limit_bytes=vmem_bytes - 4 * rows * group_elems * nodes - vmem_spare
        ),
        name="advect_helmholtz",
    )(
        velocity,
        previous.reshape(rows // 2, 2, group_elems, nodes),
        tables,
        derivative,
        stiffness,
        coupling,
        reaction,
        axial_weight,
        neighbours.T,
    )
    return out.reshape(rows, group_elems, nodes)


def solution(mesh):
    return jax.shard_map(
        functools.partial(body, mesh.shape["mode"], mesh.shape["elem"]),
        mesh=mesh,
        in_specs=(
            P(None, ("elem", "mode"), None),
            P("mode", "elem", None),
            P(),
            P(),
            P(),
            P("elem"),
            P("elem"),
            P("elem", None),
        ),
        out_specs=P("mode", "elem", None),
        check_vma=False,
    )
```

```python
import functools
import math

import jax
import jax.numpy as jnp
import ml_dtypes
import numpy as np
from jax import lax
from jax.experimental import pallas as pl
from jax.experimental.pallas import tpu as pltpu
from jax.sharding import PartitionSpec as P

dt_step = 0.5
first_weight = 0.7
second_weight = 1.1
CHUNKS = 8
PIECES = (((0, 1), (1, 4), (4, 8)), ((0, 4), (4, 6), (6, 7), (7, 8)))
vmem_bytes = 67043328
vmem_spare = 262144
MESH = pl.DeviceIdType.MESH
bf16 = jnp.bfloat16
f32 = jnp.float32


def dft_tables(planes, modes):
    half = planes // 2
    rows = np.arange(planes)
    waves = np.where(rows <= half, rows, rows - half)
    phase = (waves[:, None] * np.arange(half)[None, :]) % planes
    angles = 2.0 * math.pi / planes * phase
    table = np.where((rows <= half)[:, None], np.cos(angles), -np.sin(angles)) * planes ** (-0.5)
    table = table.reshape(modes, planes // modes // 2, 2, half).transpose(0, 2, 1, 3)
    high = table.astype(ml_dtypes.bfloat16)
    low = (table - high.astype(np.float64)).astype(ml_dtypes.bfloat16)
    return np.stack([high, low], axis=2)


def split(values):
    high = values.astype(bf16)
    low = (values - high.astype(f32)).astype(bf16)
    return high, low


def kernel(
    modes, groups, planes, elems, group_elems, rows, nodes,
    vel_hbm, prev_hbm, table_hbm, der_hbm, stiff_hbm, coup_hbm, reac_hbm, axial_hbm, near_hbm,
    outv,
    vel, prev, table, der, stiff, coup, w_slope, w_apply, folded, sent, rhs, first, inverse,
    halo_prev, halo_first, pairs, reac, axial, near,
    vel_sem, table_sem, prev_sem, small_sem, y_send, y_recv, p_send, p_recv, f_send, f_recv,
):
    half = planes // 2
    rim = group_elems // 4
    count = rows // CHUNKS
    per_parity = CHUNKS // 2
    early = min(rim, elems)
    spans = [(0, early)] + ([(early, elems)] if early < elems else [])
    faces = faces_of(group_elems)
    me = lax.axis_index("mode")
    group = lax.axis_index("elem")
    zero_slot = group_elems + 2 * rim

    def skip(mode):
        return jnp.where(mode < modes // 2, 0, elems - early)

    def element_of(mode, slot):
        if isinstance(mode, int):
            turn = 0 if mode < modes // 2 else elems - early
            return mode * elems + (slot + turn) % elems
        return mode * elems + lax.rem(slot + skip(mode), elems)

    def slot_of(element):
        mode, place = element // elems, element % elems
        turn = 0 if mode < modes // 2 else elems - early
        return mode, (place - turn) % elems

    barrier = pltpu.get_barrier_semaphore()
    for step in range(1, modes):
        pl.semaphore_signal(
            barrier, inc=1, device_id={"mode": lax.rem(me + step, modes)}, device_id_type=MESH
        )
    has_left = group > 0
    has_right = group < groups - 1

    @pl.when(has_left)
    def _():
        pl.semaphore_signal(barrier, inc=1, device_id={"elem": group - 1}, device_id_type=MESH)

    @pl.when(has_right)
    def _():
        pl.semaphore_signal(barrier, inc=1, device_id={"elem": group + 1}, device_id_type=MESH)

    der_load = pltpu.make_async_copy(der_hbm, der, small_sem.at[0])
    stiff_load = pltpu.make_async_copy(stiff_hbm, stiff, small_sem.at[1])
    coup_load = pltpu.make_async_copy(coup_hbm, coup, small_sem.at[2])

    scalar_loads = [
        pltpu.make_async_copy(src, dst, small_sem.at[3 + i])
        for i, (src, dst) in enumerate([(reac_hbm, reac), (axial_hbm, axial), (near_hbm, near)])
    ]

    def vel_load(slot):
        return pltpu.make_async_copy(
            vel_hbm.at[:, lax.rem(slot + skip(me), elems)], vel.at[slot], vel_sem.at[slot]
        )

    def table_load(step, parity):
        owner = lax.rem(me + step, modes)
        return pltpu.make_async_copy(
            table_hbm.at[owner, parity], table.at[step, parity], table_sem.at[step, parity]
        )

    def prev_load(parity, e):
        return pltpu.make_async_copy(
            prev_hbm.at[:, parity, e], prev.at[parity, e], prev_sem.at[parity, e]
        )

    steps = [*range(1, modes), 0]
    der_load.start()
    for slot in range(early):
        vel_load(slot).start()
    for parity in range(2):
        for step in range(1, modes):
            table_load(step, parity).start()
    for slot in range(early, elems):
        vel_load(slot).start()
    for parity in range(2):
        table_load(0, parity).start()
    for parity in range(2):
        for e in range(group_elems):
            prev_load(parity, e).start()
    stiff_load.start()
    coup_load.start()
    for load in scalar_loads:
        load.start()

    def halo_copies(source, halo, send, recv, c):
        right = pltpu.make_async_remote_copy(
            source(c, 0), halo.at[0, c], send.at[0, c], recv.at[0, c],
            device_id={"elem": group + 1}, device_id_type=MESH,
        )
        left = pltpu.make_async_remote_copy(
            source(c, 1), halo.at[1, c], send.at[1, c], recv.at[1, c],
            device_id={"elem": group - 1}, device_id_type=MESH,
        )
        return right, left

    def prev_rim(parity, side, i):
        return pltpu.make_async_remote_copy(
            prev_hbm.at[:, parity, (group_elems - rim) * (1 - side) + i],
            halo_prev.at[side, parity, i], p_send.at[side, parity, i], p_recv.at[side, parity, i],
            device_id={"elem": group + 1 - 2 * side}, device_id_type=MESH,
        )

    def first_copies(c):
        def source(c, side):
            return first.at[c, pl.ds((group_elems - rim) * (1 - side), rim)]

        return halo_copies(source, halo_first, f_send, f_recv, c)

    def start_halo(copies):
        right, left = copies
        pl.when(has_right)(right.start)
        pl.when(has_left)(left.start)

    def wait_halo_recv(copies):
        right, left = copies
        pl.when(has_left)(right.wait_recv)
        pl.when(has_right)(left.wait_recv)

    def wait_halo_send(copies):
        right, left = copies
        pl.when(has_right)(right.wait_send)
        pl.when(has_left)(left.wait_send)

    def each_prev_rim(parity, act_right, act_left):
        for i in range(rim):
            right, left = prev_rim(parity, 0, i), prev_rim(parity, 1, i)
            pl.when(act_right[0])(getattr(right, act_right[1]))
            pl.when(act_left[0])(getattr(left, act_left[1]))

    pl.semaphore_wait(
        barrier, modes - 1 + has_left.astype(jnp.int32) + has_right.astype(jnp.int32)
    )

    for parity in range(2):
        each_prev_rim(parity, (has_right, "start"), (has_left, "start"))

    def set_weights(ref, at, matrix):
        high, low = split(matrix.T)
        for part in range(2):
            ref[pl.ds(at + part * nodes, nodes), pl.ds(0, nodes)] = high
            ref[pl.ds(at + part * nodes, nodes), pl.ds(nodes, nodes)] = low

    der_load.wait()
    set_weights(w_slope, 0, der[...])

    block = min(256, half)

    def advect(slot):
        vel_load(slot).wait()
        for b in range(half // block):
            lower = vel[slot, pl.ds(b * block, block), :]
            upper = vel[slot, pl.ds(half + b * block, block), :]
            values = jnp.concatenate([lower, upper], axis=0)
            both = jnp.dot(
                jnp.concatenate(split(values), axis=1), w_slope[...], preferred_element_type=f32
            )
            slope = both[:, :nodes] + both[:, nodes:]
            product = values - dt_step * values * slope
            lower, upper = product[:block], product[block:]
            for parity, value in enumerate((lower + upper, lower - upper)):
                high, low = split(value)
                where = (pl.ds(b * block, block), pl.ds(slot * nodes, nodes))
                folded[(parity, 0) + where] = high
                folded[(parity, 1) + where] = low

    def transform(step, parity, start, stop, at=0, size=rows // 2):
        span = pl.ds(start * nodes, (stop - start) * nodes)
        data_high, data_low = folded[parity, 0, :, span], folded[parity, 1, :, span]
        t_high = table[step, parity, 0, pl.ds(at, size), :]
        t_low = table[step, parity, 1, pl.ds(at, size), :]
        return (
            jnp.dot(t_high, data_high, preferred_element_type=f32)
            + jnp.dot(t_low, data_high, preferred_element_type=f32)
            + jnp.dot(t_high, data_low, preferred_element_type=f32)
        )

    def put_rows(ref, parity, block_rows, start, stop, first_j=0):
        for j in range(block_rows.shape[0] // count):
            for slot in range(start, stop):
                at = (slot - start) * nodes
                ref[parity * per_parity + first_j + j, slot] = block_rows[
                    j * count : (j + 1) * count, at : at + nodes
                ]

    def y_copy(step, k, n):
        (start, stop), (at, end) = spans[k], PIECES[k][n]
        where = (pl.ds(at, end - at), pl.ds(start, stop - start))
        return pltpu.make_async_remote_copy(
            sent.at[(step - 1,) + where], rhs.at[(me,) + where],
            y_send.at[k, step - 1, n], y_recv.at[k, step - 1, n],
            device_id={"mode": lax.rem(me + step, modes)}, device_id_type=MESH,
        )

    def wait_pieces(k, c):
        for n, (at, _) in enumerate(PIECES[k]):
            @pl.when(c == at)
            def _():
                for step in range(1, modes):
                    y_copy(step, k, n).wait_recv()

    for k, (start, stop) in enumerate(spans):
        for slot in range(start, stop):
            advect(slot)
        for parity in range(2):
            for step in range(1, modes):
                if k == 0:
                    table_load(step, parity).wait()
                cuts = [0, 1, per_parity] if k == 0 and parity == 0 else [0, per_parity]
                for j, stop_j in zip(cuts, cuts[1:]):
                    part = transform(step, parity, start, stop, j * count, (stop_j - j) * count)
                    put_rows(sent.at[step - 1], parity, part, start, stop, j)
                    for n, (_, end) in enumerate(PIECES[k]):
                        if parity * per_parity + j < end <= parity * per_parity + stop_j:
                            y_copy(step, k, n).start()

    for parity in range(2):
        table_load(0, parity).wait()
        put_rows(rhs.at[me], parity, transform(0, parity, 0, elems), 0, elems)

    stiff_load.wait()
    coup_load.wait()
    for load in scalar_loads:
        load.wait()
    set_weights(w_apply, 0, stiff[...])
    for f in range(faces):
        matrix = coup[f] + coup[f + 1] if f == faces - 1 and faces < 4 else coup[f]
        set_weights(w_apply, 2 * nodes * (f + 1), matrix)
    eye = lax.broadcasted_iota(jnp.int32, (nodes, nodes), 0) == lax.broadcasted_iota(
        jnp.int32, (nodes, nodes), 1
    )
    diagonal = jnp.sum(jnp.where(eye, stiff[...], 0.0), axis=0, keepdims=True)
    pairs[zero_slot] = jnp.zeros((count, 2 * nodes), bf16)
    for parity in range(2):
        for e in range(group_elems):
            prev_load(parity, e).wait()

    def put_pair(slot, value):
        high, low = split(value)
        pairs[slot, :, pl.ds(0, nodes)] = high
        pairs[slot, :, pl.ds(nodes, nodes)] = low

    def put_halo(halo, c):
        @pl.when(has_left)
        def _():
            for i in range(rim):
                put_pair(i, halo(0, c, i))

        @pl.when(has_right)
        def _():
            for i in range(rim):
                put_pair(rim + group_elems + i, halo(1, c, i))

    def apply():
        columns = [
            jnp.concatenate([pairs[rim + e] for e in range(group_elems)], axis=0)
        ]
        for f in range(faces):
            found = []
            for e in range(group_elems):
                n = near[f, e]
                slot = jnp.clip(n - group * group_elems + rim, 0, zero_slot - 1)
                slot = jnp.where(n >= 0, slot, zero_slot)
                found.append(pairs[slot])
            columns.append(jnp.concatenate(found, axis=0))
        both = jnp.dot(
            jnp.concatenate(columns, axis=1), w_apply[...], preferred_element_type=f32
        )
        return both[:, :nodes] + both[:, nodes:]

    def prev_rows(c, e):
        return prev[c // per_parity, e, pl.ds((c % per_parity) * count, count), :]

    def prev_halo_rows(side, c, i):
        return halo_prev[side, c // per_parity, i, pl.ds((c % per_parity) * count, count), :]

    def shifts(c):
        places = lax.broadcasted_iota(jnp.int32, (count, nodes), 0)
        row = me * rows + 2 * ((c % per_parity) * count + places) + c // per_parity
        wave = jnp.where(row <= half, row, row - half).astype(f32)
        return 4.0 * (wave / half) ** 2

    def complete(c, mode, slot, e):
        first[c, e] = first[c, e] + first_weight * inverse[c, e] * rhs[mode, c, slot]

    def first_sweep(c, carry):
        for e in range(group_elems):
            put_pair(rim + e, prev_rows(c, e))
        for parity in range(2):
            pl.when(c == parity * per_parity)(
                lambda: each_prev_rim(parity, (has_left, "wait_recv"), (has_right, "wait_recv"))
            )
        put_halo(prev_halo_rows, c)
        applied = apply()
        shift = shifts(c)
        for e in range(group_elems):
            scaling = reac[e] + shift * axial[e]
            recip = 1.0 / (diagonal + scaling)
            inverse[c, e] = recip
            value = prev_rows(c, e)
            part = applied[e * count : (e + 1) * count]
            first[c, e] = value - first_weight * recip * (part + scaling * value)
        for slot in range(early, elems):
            complete(c, me, slot, element_of(me, slot))
        wait_pieces(0, c)
        for mode in range(modes):
            for slot in range(early):
                complete(c, mode, slot, element_of(mode, slot))
        start_halo(first_copies(c))
        return carry

    def second_sweep(c, carry):
        for mode in range(modes):
            for slot in range(early):
                e = element_of(mode, slot)
                put_pair(rim + e, first[c, e])
        for slot in range(early, elems):
            e = element_of(me, slot)
            put_pair(rim + e, first[c, e])
        wait_halo_recv(first_copies(c))
        put_halo(lambda side, c, i: halo_first[side, c, i], c)
        if early < elems:
            wait_pieces(1, c)
            for step in range(1, modes):
                mode = lax.rem(me + step, modes)
                for slot in range(early, elems):
                    e = element_of(mode, slot)
                    complete(c, mode, slot, e)
                    put_pair(rim + e, first[c, e])
        applied = apply()
        shift = shifts(c)
        for e in range(group_elems):
            mode, slot = slot_of(e)
            scaling = reac[e] + shift * axial[e]
            value = first[c, e]
            part = applied[e * count : (e + 1) * count]
            start = (2 * (c % per_parity) * count + c // per_parity) * group_elems + e
            outv[pl.ds(start, count, stride=2 * group_elems), :] = value + second_weight * inverse[
                c, e
            ] * (rhs[mode, c, slot] - (part + scaling * value))
        return carry

    lax.fori_loop(0, CHUNKS, first_sweep, 0)
    lax.fori_loop(0, CHUNKS, second_sweep, 0)

    def finish(c, carry):
        wait_halo_send(first_copies(c))
        return carry

    lax.fori_loop(0, CHUNKS, finish, 0)
    for parity in range(2):
        each_prev_rim(parity, (has_right, "wait_send"), (has_left, "wait_send"))
    for k in range(len(spans)):
        for n in range(len(PIECES[k])):
            for step in range(1, modes):
                y_copy(step, k, n).wait_send()


def faces_of(group_elems):
    return 3 if group_elems // 4 == 2 else 4


def body(modes, groups, velocity, previous, derivative, stiffness, coupling, reaction, axial_weight, neighbours):
    planes, elems, nodes = velocity.shape
    rows, group_elems, _ = previous.shape
    half = planes // 2
    rim = group_elems // 4
    count = rows // CHUNKS
    tables = jnp.asarray(dft_tables(planes, modes))
    run = functools.partial(kernel, modes, groups, planes, elems, group_elems, rows, nodes)
    anywhere = pl.BlockSpec(memory_space=pltpu.HBM)
    dma = pltpu.SemaphoreType.DMA
    taps = faces_of(group_elems) + 1
    scratch = [
        pltpu.VMEM((elems, planes, nodes), f32),
        pltpu.VMEM((2, group_elems, rows // 2, nodes), f32),
        pltpu.VMEM(tables.shape, bf16),
        pltpu.VMEM((nodes, nodes), f32),
        pltpu.VMEM((nodes, nodes), f32),
        pltpu.VMEM((4, nodes, nodes), f32),
        pltpu.VMEM((2 * nodes, 2 * nodes), bf16),
        pltpu.VMEM((taps * 2 * nodes, 2 * nodes), bf16),
        pltpu.VMEM((2, 2, half, elems * nodes), bf16),
        pltpu.VMEM((modes - 1, CHUNKS, elems, count, nodes), f32),
        pltpu.VMEM((modes, CHUNKS, elems, count, nodes), f32),
        pltpu.VMEM((CHUNKS, group_elems, count, nodes), f32),
        pltpu.VMEM((CHUNKS, group_elems, count, nodes), f32),
        pltpu.VMEM((2, 2, rim, rows // 2, nodes), f32),
        pltpu.VMEM((2, CHUNKS, rim, count, nodes), f32),
        pltpu.VMEM((group_elems + 2 * rim + 1, count, 2 * nodes), bf16),
        pltpu.SMEM((group_elems,), f32),
        pltpu.SMEM((group_elems,), f32),
        pltpu.SMEM((4, group_elems), jnp.int32),
    ]
    semaphores = [
        dma((elems,)),
        dma((modes, 2)),
        dma((2, group_elems)),
        dma((6,)),
        dma((2, modes - 1, CHUNKS)),
        dma((2, modes - 1, CHUNKS)),
        dma((2, 2, rim)),
        dma((2, 2, rim)),
        dma((2, CHUNKS)),
        dma((2, CHUNKS)),
    ]
    out = pl.pallas_call(
        run,
        out_shape=pltpu.VMEM((rows * group_elems, nodes), f32),
        in_specs=[anywhere] * 9,
        out_specs=pl.BlockSpec(memory_space=pltpu.VMEM),
        scratch_shapes=scratch + semaphores,
        compiler_params=pltpu.CompilerParams(
            collective_id=0, has_side_effects=True, vmem_limit_bytes=vmem_bytes - 4 * rows * group_elems * nodes - vmem_spare
        ),
        name="advect_helmholtz",
    )(
        velocity,
        previous.reshape(rows // 2, 2, group_elems, nodes),
        tables,
        derivative,
        stiffness,
        coupling,
        reaction,
        axial_weight,
        neighbours.T,
    )
    return out.reshape(rows, group_elems, nodes)


def solution(mesh):
    return jax.shard_map(
        functools.partial(body, mesh.shape["mode"], mesh.shape["elem"]),
        mesh=mesh,
        in_specs=(
            P(None, ("elem", "mode"), None),
            P("mode", "elem", None),
            P(),
            P(),
            P(),
            P("elem"),
            P("elem"),
            P("elem", None),
        ),
        out_specs=P("mode", "elem", None),
        check_vma=False,
    )
```

```python
import functools
import math

import jax
import jax.numpy as jnp
import ml_dtypes
import numpy as np
from jax import lax
from jax.experimental import pallas as pl
from jax.experimental.pallas import tpu as pltpu
from jax.sharding import PartitionSpec as P

dt_step = 0.5
first_weight = 0.7
second_weight = 1.1
CHUNKS = 8
LEAD_CUTS = (0, 1, 4, 8)
EARLY_CUTS = (0, 4, 8)
REST_AT = 0
LATE_CUTS = (0, 4, 6, 7, 8)
vmem_bytes = 67043328
vmem_spare = 262144
MESH = pl.DeviceIdType.MESH
bf16 = jnp.bfloat16
f32 = jnp.float32


def dft_tables(planes, modes):
    half = planes // 2
    rows = np.arange(planes)
    waves = np.where(rows <= half, rows, rows - half)
    phase = (waves[:, None] * np.arange(half)[None, :]) % planes
    angles = 2.0 * math.pi / planes * phase
    table = np.where((rows <= half)[:, None], np.cos(angles), -np.sin(angles)) * planes ** (-0.5)
    table = table.reshape(modes, planes // modes // 2, 2, half).transpose(0, 2, 1, 3)
    high = table.astype(ml_dtypes.bfloat16)
    low = (table - high.astype(np.float64)).astype(ml_dtypes.bfloat16)
    return np.stack([high, low], axis=2)


def split(values):
    high = values.astype(bf16)
    low = (values - high.astype(f32)).astype(bf16)
    return high, low


def kernel(
    modes, groups, planes, elems, group_elems, rows, nodes,
    vel_hbm, prev_hbm, table_hbm, der_hbm, stiff_hbm, coup_hbm, reac_hbm, axial_hbm, near_hbm,
    outv,
    vel, prev, table, der, stiff, coup, w_slope, w_apply, folded, sent, rhs, first, inverse,
    halo_prev, halo_first, pairs, reac, axial, near,
    lead_sem, vel_sem, table_sem, prev_sem, small_sem, y_send, y_recv, p_send, p_recv, f_send, f_recv,
):
    half = planes // 2
    rim = group_elems // 4
    count = rows // CHUNKS
    per_parity = CHUNKS // 2
    early = min(rim, elems)
    spans = [
        (start, stop, cuts)
        for start, stop, cuts in [
            (0, 1, LEAD_CUTS), (1, early, EARLY_CUTS), (early, elems, LATE_CUTS)
        ]
        if start < stop
    ]
    faces = faces_of(group_elems)
    me = lax.axis_index("mode")
    group = lax.axis_index("elem")
    zero_slot = group_elems + 2 * rim

    def skip(mode):
        return jnp.where(mode < modes // 2, 0, elems - early)

    def element_of(mode, slot):
        if isinstance(mode, int):
            turn = 0 if mode < modes // 2 else elems - early
            return mode * elems + (slot + turn) % elems
        return mode * elems + lax.rem(slot + skip(mode), elems)

    def slot_of(element):
        mode, place = element // elems, element % elems
        turn = 0 if mode < modes // 2 else elems - early
        return mode, (place - turn) % elems

    der_load = pltpu.make_async_copy(der_hbm, der, small_sem.at[0])
    stiff_load = pltpu.make_async_copy(stiff_hbm, stiff, small_sem.at[1])
    coup_load = pltpu.make_async_copy(coup_hbm, coup, small_sem.at[2])

    scalar_loads = [
        pltpu.make_async_copy(src, dst, small_sem.at[3 + i])
        for i, (src, dst) in enumerate([(reac_hbm, reac), (axial_hbm, axial), (near_hbm, near)])
    ]

    block = min(256, half)

    def vel_load(slot):
        return pltpu.make_async_copy(
            vel_hbm.at[:, lax.rem(slot + skip(me), elems)], vel.at[slot], vel_sem.at[slot]
        )

    def lead_load(b, side):
        where = pl.ds(side * half + b * block, block)
        return pltpu.make_async_copy(
            vel_hbm.at[where, skip(me)], vel.at[0, where], lead_sem.at[b, side]
        )

    def table_load(step, parity):
        owner = lax.rem(me + step, modes)
        return pltpu.make_async_copy(
            table_hbm.at[owner, parity], table.at[step, parity], table_sem.at[step, parity]
        )

    def prev_load(parity, e):
        return pltpu.make_async_copy(
            prev_hbm.at[:, parity, e], prev.at[parity, e], prev_sem.at[parity, e]
        )

    steps = [*range(1, modes), 0]
    der_load.start()
    for b in range(half // block):
        for side in range(2):
            lead_load(b, side).start()
    for step in range(1, modes):
        table_load(step, 0).start()
    for slot in range(1, early):
        vel_load(slot).start()
    for step in range(1, modes):
        table_load(step, 1).start()
    def start_rest():
        for slot in range(early, elems):
            vel_load(slot).start()
        for parity in range(2):
            table_load(0, parity).start()
        for parity in range(2):
            for e in range(group_elems):
                prev_load(parity, e).start()
        stiff_load.start()
        coup_load.start()
        for load in scalar_loads:
            load.start()

    barrier = pltpu.get_barrier_semaphore()
    for step in range(1, modes):
        pl.semaphore_signal(
            barrier, inc=1, device_id={"mode": lax.rem(me + step, modes)}, device_id_type=MESH
        )
    has_left = group > 0
    has_right = group < groups - 1

    @pl.when(has_left)
    def _():
        pl.semaphore_signal(barrier, inc=1, device_id={"elem": group - 1}, device_id_type=MESH)

    @pl.when(has_right)
    def _():
        pl.semaphore_signal(barrier, inc=1, device_id={"elem": group + 1}, device_id_type=MESH)

    def halo_copies(source, halo, send, recv, c):
        right = pltpu.make_async_remote_copy(
            source(c, 0), halo.at[0, c], send.at[0, c], recv.at[0, c],
            device_id={"elem": group + 1}, device_id_type=MESH,
        )
        left = pltpu.make_async_remote_copy(
            source(c, 1), halo.at[1, c], send.at[1, c], recv.at[1, c],
            device_id={"elem": group - 1}, device_id_type=MESH,
        )
        return right, left

    def prev_rim(parity, side, i):
        return pltpu.make_async_remote_copy(
            prev_hbm.at[:, parity, (group_elems - rim) * (1 - side) + i],
            halo_prev.at[side, parity, i], p_send.at[side, parity, i], p_recv.at[side, parity, i],
            device_id={"elem": group + 1 - 2 * side}, device_id_type=MESH,
        )

    def first_copies(c):
        def source(c, side):
            return first.at[c, pl.ds((group_elems - rim) * (1 - side), rim)]

        return halo_copies(source, halo_first, f_send, f_recv, c)

    def wait_halo_recv(copies):
        right, left = copies
        pl.when(has_left)(right.wait_recv)
        pl.when(has_right)(left.wait_recv)

    def wait_halo_send(copies):
        right, left = copies
        pl.when(has_right)(right.wait_send)
        pl.when(has_left)(left.wait_send)

    def each_prev_rim(parity, act_right, act_left):
        for i in range(rim):
            right, left = prev_rim(parity, 0, i), prev_rim(parity, 1, i)
            pl.when(act_right[0])(getattr(right, act_right[1]))
            pl.when(act_left[0])(getattr(left, act_left[1]))

    far_right = jnp.logical_and(has_right, lax.rem(group, 4) == 3)
    far_left = jnp.logical_and(has_left, lax.rem(group, 4) == 0)
    near_right = jnp.logical_and(has_right, lax.rem(group, 4) != 3)
    near_left = jnp.logical_and(has_left, lax.rem(group, 4) != 0)
    left_local = me == 0
    right_local = me == modes - 1
    held_back = lax.rem(group, 2) == 1

    def set_weights(ref, at, matrix):
        high, low = split(matrix.T)
        for part in range(2):
            ref[pl.ds(at + part * nodes, nodes), pl.ds(0, nodes)] = high
            ref[pl.ds(at + part * nodes, nodes), pl.ds(nodes, nodes)] = low

    der_load.wait()
    set_weights(w_slope, 0, der[...])

    def advect(slot):
        if slot > 0:
            vel_load(slot).wait()
        for b in range(half // block):
            if slot == 0:
                lead_load(b, 0).wait()
                lead_load(b, 1).wait()
            lower = vel[slot, pl.ds(b * block, block), :]
            upper = vel[slot, pl.ds(half + b * block, block), :]
            values = jnp.concatenate([lower, upper], axis=0)
            both = jnp.dot(
                jnp.concatenate(split(values), axis=1), w_slope[...], preferred_element_type=f32
            )
            slope = both[:, :nodes] + both[:, nodes:]
            product = values - dt_step * values * slope
            lower, upper = product[:block], product[block:]
            for parity, value in enumerate((lower + upper, lower - upper)):
                high, low = split(value)
                where = (pl.ds(b * block, block), pl.ds(slot * nodes, nodes))
                folded[(parity, 0) + where] = high
                folded[(parity, 1) + where] = low

    def transform(step, parity, start, stop, at=0, size=rows // 2):
        span = pl.ds(start * nodes, (stop - start) * nodes)
        data_high, data_low = folded[parity, 0, :, span], folded[parity, 1, :, span]
        t_high = table[step, parity, 0, pl.ds(at, size), :]
        t_low = table[step, parity, 1, pl.ds(at, size), :]
        return (
            jnp.dot(t_high, data_high, preferred_element_type=f32)
            + jnp.dot(t_low, data_high, preferred_element_type=f32)
            + jnp.dot(t_high, data_low, preferred_element_type=f32)
        )

    def put_rows(ref, parity, block_rows, start, stop, first_j=0):
        for j in range(block_rows.shape[0] // count):
            for slot in range(start, stop):
                at = (slot - start) * nodes
                ref[parity * per_parity + first_j + j, slot] = block_rows[
                    j * count : (j + 1) * count, at : at + nodes
                ]

    def y_copy(step, k, n):
        start, stop, cuts = spans[k]
        where = (pl.ds(cuts[n], cuts[n + 1] - cuts[n]), pl.ds(start, stop - start))
        return pltpu.make_async_remote_copy(
            sent.at[(step - 1,) + where], rhs.at[(me,) + where],
            y_send.at[k, step - 1, n], y_recv.at[k, step - 1, n],
            device_id={"mode": lax.rem(me + step, modes)}, device_id_type=MESH,
        )

    def start_pieces(k, at=0, end=CHUNKS):
        for n, cut in enumerate(spans[k][2][1:]):
            if at < cut <= end:
                for step in range(1, modes):
                    y_copy(step, k, n).start()

    def wait_pieces(late, c, begin=0, end=CHUNKS, also=True):
        for at in range(begin, end):
            due = [
                (k, n)
                for k, (start, _, cuts) in enumerate(spans)
                for n, cut in enumerate(cuts[:-1])
                if cut == at and (start >= early) == late
            ]
            if due:
                @pl.when(jnp.logical_and(c == at, also))
                def _():
                    for k, n in due:
                        for step in range(1, modes):
                            y_copy(step, k, n).wait_recv()

    for k, (start, stop, _) in enumerate(spans):
        for slot in range(start, stop):
            advect(slot)
        if k == 0:
            pl.semaphore_wait(
                barrier, modes - 1 + has_left.astype(jnp.int32) + has_right.astype(jnp.int32)
            )

            each_prev_rim(0, (has_right, "start"), (has_left, "start"))
            each_prev_rim(1, (near_right, "start"), (near_left, "start"))
        for parity in range(2):
            if k == 0:
                for step in range(1, modes):
                    table_load(step, parity).wait()
            cuts = [0, 1, per_parity] if k == 0 and parity == 0 else [0, per_parity]
            for j, stop_j in zip(cuts, cuts[1:]):
                for step in range(1, modes):
                    part = transform(step, parity, start, stop, j * count, (stop_j - j) * count)
                    put_rows(sent.at[step - 1], parity, part, start, stop, j)
                at, end = parity * per_parity + j, parity * per_parity + stop_j
                if start < early:
                    start_pieces(k, at, end)
                else:
                    pl.when(jnp.logical_not(held_back))(lambda: start_pieces(k, at, end))
                if k == 0 and at == REST_AT:
                    start_rest()

    each_prev_rim(1, (far_right, "start"), (far_left, "start"))
    for parity in range(2):
        table_load(0, parity).wait()
        put_rows(rhs.at[me], parity, transform(0, parity, 0, elems), 0, elems)

    stiff_load.wait()
    coup_load.wait()
    for load in scalar_loads:
        load.wait()
    set_weights(w_apply, 0, stiff[...])
    for f in range(faces):
        matrix = coup[f] + coup[f + 1] if f == faces - 1 and faces < 4 else coup[f]
        set_weights(w_apply, 2 * nodes * (f + 1), matrix)
    eye = lax.broadcasted_iota(jnp.int32, (nodes, nodes), 0) == lax.broadcasted_iota(
        jnp.int32, (nodes, nodes), 1
    )
    diagonal = jnp.sum(jnp.where(eye, stiff[...], 0.0), axis=0, keepdims=True)
    pairs[zero_slot] = jnp.zeros((count, 2 * nodes), bf16)
    for parity in range(2):
        for e in range(group_elems):
            prev_load(parity, e).wait()

    def put_pair(slot, value):
        high, low = split(value)
        pairs[slot, :, pl.ds(0, nodes)] = high
        pairs[slot, :, pl.ds(nodes, nodes)] = low

    def put_halo(halo, c):
        @pl.when(has_left)
        def _():
            for i in range(rim):
                put_pair(i, halo(0, c, i))

        @pl.when(has_right)
        def _():
            for i in range(rim):
                put_pair(rim + group_elems + i, halo(1, c, i))

    def apply():
        columns = [
            jnp.concatenate([pairs[rim + e] for e in range(group_elems)], axis=0)
        ]
        for f in range(faces):
            found = []
            for e in range(group_elems):
                n = near[f, e]
                slot = jnp.clip(n - group * group_elems + rim, 0, zero_slot - 1)
                slot = jnp.where(n >= 0, slot, zero_slot)
                found.append(pairs[slot])
            columns.append(jnp.concatenate(found, axis=0))
        both = jnp.dot(
            jnp.concatenate(columns, axis=1), w_apply[...], preferred_element_type=f32
        )
        return both[:, :nodes] + both[:, nodes:]

    def prev_rows(c, e):
        return prev[c // per_parity, e, pl.ds((c % per_parity) * count, count), :]

    def prev_halo_rows(side, c, i):
        return halo_prev[side, c // per_parity, i, pl.ds((c % per_parity) * count, count), :]

    def shifts(c):
        places = lax.broadcasted_iota(jnp.int32, (count, nodes), 0)
        row = me * rows + 2 * ((c % per_parity) * count + places) + c // per_parity
        wave = jnp.where(row <= half, row, row - half).astype(f32)
        return 4.0 * (wave / half) ** 2

    def complete(c, mode, slot, e):
        first[c, e] = first[c, e] + first_weight * inverse[c, e] * rhs[mode, c, slot]

    def first_sweep(c, carry):
        for e in range(group_elems):
            put_pair(rim + e, prev_rows(c, e))
        for parity in range(2):
            pl.when(c == parity * per_parity)(
                lambda: each_prev_rim(parity, (has_left, "wait_recv"), (has_right, "wait_recv"))
            )
        put_halo(prev_halo_rows, c)
        applied = apply()
        shift = shifts(c)
        for e in range(group_elems):
            scaling = reac[e] + shift * axial[e]
            recip = 1.0 / (diagonal + scaling)
            inverse[c, e] = recip
            value = prev_rows(c, e)
            part = applied[e * count : (e + 1) * count]
            first[c, e] = value - first_weight * recip * (part + scaling * value)
        for slot in range(elems):
            complete(c, me, slot, element_of(me, slot))
        right, left = first_copies(c)
        pl.when(jnp.logical_and(has_right, right_local))(right.start)
        pl.when(jnp.logical_and(has_left, left_local))(left.start)
        return carry

    def finish_rims(c, carry):
        wait_pieces(False, c, 0, per_parity)
        wait_pieces(False, c, per_parity, CHUNKS, jnp.logical_not(held_back))
        for step in range(1, modes):
            mode = lax.rem(me + step, modes)
            for slot in range(early):
                complete(c, mode, slot, element_of(mode, slot))
        right, left = first_copies(c)
        pl.when(jnp.logical_and(has_right, jnp.logical_not(right_local)))(right.start)
        pl.when(jnp.logical_and(has_left, jnp.logical_not(left_local)))(left.start)
        return carry

    def first_half(parity, carry):
        at = parity * per_parity
        lax.fori_loop(at, at + per_parity, first_sweep, 0)
        lax.fori_loop(at, at + per_parity, finish_rims, 0)

        @pl.when(jnp.logical_and(held_back, parity == 0))
        def _():
            wait_pieces(False, per_parity)
            if early < elems:
                start_pieces(len(spans) - 1)

        return carry

    def second_sweep(c, carry):
        for mode in range(modes):
            for slot in range(early):
                e = element_of(mode, slot)
                put_pair(rim + e, first[c, e])
        for slot in range(early, elems):
            e = element_of(me, slot)
            put_pair(rim + e, first[c, e])
        wait_halo_recv(first_copies(c))
        put_halo(lambda side, c, i: halo_first[side, c, i], c)
        if early < elems:
            wait_pieces(True, c)
            for step in range(1, modes):
                mode = lax.rem(me + step, modes)
                for slot in range(early, elems):
                    e = element_of(mode, slot)
                    complete(c, mode, slot, e)
                    put_pair(rim + e, first[c, e])
        applied = apply()
        shift = shifts(c)
        for e in range(group_elems):
            mode, slot = slot_of(e)
            scaling = reac[e] + shift * axial[e]
            value = first[c, e]
            part = applied[e * count : (e + 1) * count]
            start = (2 * (c % per_parity) * count + c // per_parity) * group_elems + e
            outv[pl.ds(start, count, stride=2 * group_elems), :] = value + second_weight * inverse[
                c, e
            ] * (rhs[mode, c, slot] - (part + scaling * value))
        return carry

    lax.fori_loop(0, 2, first_half, 0)
    lax.fori_loop(0, CHUNKS, second_sweep, 0)

    def finish(c, carry):
        wait_halo_send(first_copies(c))
        return carry

    lax.fori_loop(0, CHUNKS, finish, 0)
    for parity in range(2):
        each_prev_rim(parity, (has_right, "wait_send"), (has_left, "wait_send"))
    for k in range(len(spans)):
        for n in range(len(spans[k][2]) - 1):
            for step in range(1, modes):
                y_copy(step, k, n).wait_send()


def faces_of(group_elems):
    return 3 if group_elems // 4 == 2 else 4


def body(modes, groups, velocity, previous, derivative, stiffness, coupling, reaction, axial_weight, neighbours):
    planes, elems, nodes = velocity.shape
    rows, group_elems, _ = previous.shape
    half = planes // 2
    rim = group_elems // 4
    count = rows // CHUNKS
    tables = jnp.asarray(dft_tables(planes, modes))
    run = functools.partial(kernel, modes, groups, planes, elems, group_elems, rows, nodes)
    anywhere = pl.BlockSpec(memory_space=pltpu.HBM)
    dma = pltpu.SemaphoreType.DMA
    taps = faces_of(group_elems) + 1
    scratch = [
        pltpu.VMEM((elems, planes, nodes), f32),
        pltpu.VMEM((2, group_elems, rows // 2, nodes), f32),
        pltpu.VMEM(tables.shape, bf16),
        pltpu.VMEM((nodes, nodes), f32),
        pltpu.VMEM((nodes, nodes), f32),
        pltpu.VMEM((4, nodes, nodes), f32),
        pltpu.VMEM((2 * nodes, 2 * nodes), bf16),
        pltpu.VMEM((taps * 2 * nodes, 2 * nodes), bf16),
        pltpu.VMEM((2, 2, half, elems * nodes), bf16),
        pltpu.VMEM((modes - 1, CHUNKS, elems, count, nodes), f32),
        pltpu.VMEM((modes, CHUNKS, elems, count, nodes), f32),
        pltpu.VMEM((CHUNKS, group_elems, count, nodes), f32),
        pltpu.VMEM((CHUNKS, group_elems, count, nodes), f32),
        pltpu.VMEM((2, 2, rim, rows // 2, nodes), f32),
        pltpu.VMEM((2, CHUNKS, rim, count, nodes), f32),
        pltpu.VMEM((group_elems + 2 * rim + 1, count, 2 * nodes), bf16),
        pltpu.SMEM((group_elems,), f32),
        pltpu.SMEM((group_elems,), f32),
        pltpu.SMEM((4, group_elems), jnp.int32),
    ]
    semaphores = [
        dma((half // min(256, half), 2)),
        dma((elems,)),
        dma((modes, 2)),
        dma((2, group_elems)),
        dma((6,)),
        dma((3, modes - 1, CHUNKS)),
        dma((3, modes - 1, CHUNKS)),
        dma((2, 2, rim)),
        dma((2, 2, rim)),
        dma((2, CHUNKS)),
        dma((2, CHUNKS)),
    ]
    out = pl.pallas_call(
        run,
        out_shape=pltpu.VMEM((rows * group_elems, nodes), f32),
        in_specs=[anywhere] * 9,
        out_specs=pl.BlockSpec(memory_space=pltpu.VMEM),
        scratch_shapes=scratch + semaphores,
        compiler_params=pltpu.CompilerParams(
            collective_id=0, has_side_effects=True, vmem_limit_bytes=vmem_bytes - 4 * rows * group_elems * nodes - vmem_spare
        ),
        name="advect_helmholtz",
    )(
        velocity,
        previous.reshape(rows // 2, 2, group_elems, nodes),
        tables,
        derivative,
        stiffness,
        coupling,
        reaction,
        axial_weight,
        neighbours.T,
    )
    return out.reshape(rows, group_elems, nodes)


def solution(mesh):
    return jax.shard_map(
        functools.partial(body, mesh.shape["mode"], mesh.shape["elem"]),
        mesh=mesh,
        in_specs=(
            P(None, ("elem", "mode"), None),
            P("mode", "elem", None),
            P(),
            P(),
            P(),
            P("elem"),
            P("elem"),
            P("elem", None),
        ),
        out_specs=P("mode", "elem", None),
        check_vma=False,
    )
```

```python
import functools
import math

import jax
import jax.numpy as jnp
import ml_dtypes
import numpy as np
from jax import lax
from jax.experimental import pallas as pl
from jax.experimental.pallas import tpu as pltpu
from jax.sharding import PartitionSpec as P

dt_step = 0.5
first_weight = 0.7
second_weight = 1.1
CHUNKS = 8
LEAD_CUTS = (0, 1, 4, 8)
EARLY_CUTS = (0, 4, 8)
REST_AT = 0
LATE_CUTS = (0, 4, 6, 7, 8)
PIECES = 9
vmem_bytes = 67043328
vmem_spare = 262144
MESH = pl.DeviceIdType.MESH
bf16 = jnp.bfloat16
f32 = jnp.float32


def dft_tables(planes, modes):
    half = planes // 2
    rows = np.arange(planes)
    waves = np.where(rows <= half, rows, rows - half)
    phase = (waves[:, None] * np.arange(half)[None, :]) % planes
    angles = 2.0 * math.pi / planes * phase
    table = np.where((rows <= half)[:, None], np.cos(angles), -np.sin(angles)) * planes ** (-0.5)
    table = table.reshape(modes, planes // modes // 2, 2, half).transpose(0, 2, 1, 3)
    high = table.astype(ml_dtypes.bfloat16)
    low = (table - high.astype(np.float64)).astype(ml_dtypes.bfloat16)
    return np.stack([high, low], axis=2)


def split(values):
    high = values.astype(bf16)
    low = (values - high.astype(f32)).astype(bf16)
    return high, low


def kernel(
    modes, groups, planes, elems, group_elems, rows, nodes,
    vel_hbm, prev_hbm, table_hbm, der_hbm, stiff_hbm, coup_hbm, reac_hbm, axial_hbm, near_hbm,
    outv,
    vel, prev, table, der, taps, w_slope, w_apply, folded, sent, rhs, first, inverse,
    halo_prev, halo_first, pairs, weights, near,
    lead_sem, vel_sem, table_sem, small_sem, y_send, y_recv, p_send, p_recv, f_send, f_recv,
):
    half = planes // 2
    rim = group_elems // 4
    count = rows // CHUNKS
    per_parity = CHUNKS // 2
    early = min(rim, elems)
    spans = [
        (start, stop, cuts)
        for start, stop, cuts in [
            (0, 1, LEAD_CUTS), (1, early, EARLY_CUTS), (early, elems, LATE_CUTS)
        ]
        if start < stop
    ]
    first_piece = [sum(len(cuts) - 1 for _, _, cuts in spans[:k]) for k in range(len(spans) + 1)]
    faces = faces_of(group_elems)
    me = lax.axis_index("mode")
    group = lax.axis_index("elem")
    zero_slot = group_elems + 2 * rim

    def skip(mode):
        return jnp.where(mode < modes // 2, 0, elems - early)

    def element_of(mode, slot):
        if isinstance(mode, int):
            turn = 0 if mode < modes // 2 else elems - early
            return mode * elems + (slot + turn) % elems
        return mode * elems + lax.rem(slot + skip(mode), elems)

    def slot_of(element):
        mode, place = element // elems, element % elems
        turn = 0 if mode < modes // 2 else elems - early
        return mode, (place - turn) % elems

    der_load = pltpu.make_async_copy(der_hbm, der, small_sem.at[0])
    stiff_load = pltpu.make_async_copy(stiff_hbm, taps.at[0], small_sem.at[1])
    coup_load = pltpu.make_async_copy(coup_hbm, taps.at[pl.ds(1, 4)], small_sem.at[1])

    scalar_loads = [
        pltpu.make_async_copy(src, dst, small_sem.at[i])
        for i, src, dst in [
            (2, reac_hbm, weights.at[0]), (2, axial_hbm, weights.at[1]), (3, near_hbm, near)
        ]
    ]

    block = min(256, half)

    def vel_load(slot):
        return pltpu.make_async_copy(
            vel_hbm.at[:, lax.rem(slot + skip(me), elems)], vel.at[slot], vel_sem.at[min(slot, early)]
        )

    def lead_load(b, side):
        where = pl.ds(side * half + b * block, block)
        return pltpu.make_async_copy(
            vel_hbm.at[where, skip(me)], vel.at[0, where], lead_sem.at[b]
        )

    def wait_whole(ref, sem):
        pltpu.make_async_copy(ref, ref, sem).wait()

    def table_load(step, parity):
        owner = lax.rem(me + step, modes)
        return pltpu.make_async_copy(
            table_hbm.at[owner, parity], table.at[step, parity], table_sem.at[2 * step - 1 + parity]
        )

    own_table_load = pltpu.make_async_copy(table_hbm.at[me], table.at[0], table_sem.at[0])

    def prev_load(parity, e):
        return pltpu.make_async_copy(
            prev_hbm.at[:, parity, e], prev.at[parity, e], small_sem.at[4]
        )

    steps = [*range(1, modes), 0]
    der_load.start()
    for b in range(half // block):
        for side in range(2):
            lead_load(b, side).start()
    for step in range(1, modes):
        table_load(step, 0).start()
    for slot in range(1, early):
        vel_load(slot).start()
    for step in range(1, modes):
        table_load(step, 1).start()
    def start_rest():
        for slot in range(early, elems):
            vel_load(slot).start()
        own_table_load.start()
        for parity in range(2):
            for e in range(group_elems):
                prev_load(parity, e).start()
        stiff_load.start()
        coup_load.start()
        for load in scalar_loads:
            load.start()

    barrier = pltpu.get_barrier_semaphore()
    for step in range(1, modes):
        pl.semaphore_signal(
            barrier, inc=1, device_id={"mode": lax.rem(me + step, modes)}, device_id_type=MESH
        )
    has_left = group > 0
    has_right = group < groups - 1

    @pl.when(has_left)
    def _():
        pl.semaphore_signal(barrier, inc=1, device_id={"elem": group - 1}, device_id_type=MESH)

    @pl.when(has_right)
    def _():
        pl.semaphore_signal(barrier, inc=1, device_id={"elem": group + 1}, device_id_type=MESH)

    def halo_copies(source, halo, send, recv, c):
        right = pltpu.make_async_remote_copy(
            source(c, 0), halo.at[0, c], send.at[0], recv.at[0, c],
            device_id={"elem": group + 1}, device_id_type=MESH,
        )
        left = pltpu.make_async_remote_copy(
            source(c, 1), halo.at[1, c], send.at[1], recv.at[1, c],
            device_id={"elem": group - 1}, device_id_type=MESH,
        )
        return right, left

    def prev_rim(parity, side, i):
        return pltpu.make_async_remote_copy(
            prev_hbm.at[:, parity, (group_elems - rim) * (1 - side) + i],
            halo_prev.at[side, parity, i], p_send.at[side], p_recv.at[side, parity],
            device_id={"elem": group + 1 - 2 * side}, device_id_type=MESH,
        )

    def wait_prev_rims(parity):
        pl.when(has_left)(lambda: wait_whole(halo_prev.at[0, parity], p_recv.at[0, parity]))
        pl.when(has_right)(lambda: wait_whole(halo_prev.at[1, parity], p_recv.at[1, parity]))

    def first_copies(c):
        def source(c, side):
            return first.at[c, pl.ds((group_elems - rim) * (1 - side), rim)]

        return halo_copies(source, halo_first, f_send, f_recv, c)

    def wait_halo_recv(copies):
        right, left = copies
        pl.when(has_left)(right.wait_recv)
        pl.when(has_right)(left.wait_recv)

    def each_prev_rim(parity, act_right, act_left):
        for i in range(rim):
            right, left = prev_rim(parity, 0, i), prev_rim(parity, 1, i)
            pl.when(act_right[0])(getattr(right, act_right[1]))
            pl.when(act_left[0])(getattr(left, act_left[1]))

    far_right = jnp.logical_and(has_right, lax.rem(group, 4) == 3)
    far_left = jnp.logical_and(has_left, lax.rem(group, 4) == 0)
    near_right = jnp.logical_and(has_right, lax.rem(group, 4) != 3)
    near_left = jnp.logical_and(has_left, lax.rem(group, 4) != 0)
    left_local = me == 0
    right_local = me == modes - 1
    held_back = lax.rem(group, 2) == 1

    def set_weights(ref, at, matrix):
        high, low = split(matrix.T)
        for part in range(2):
            ref[pl.ds(at + part * nodes, nodes), pl.ds(0, nodes)] = high
            ref[pl.ds(at + part * nodes, nodes), pl.ds(nodes, nodes)] = low

    der_load.wait()
    set_weights(w_slope, 0, der[...])

    def advect(slot):
        if 0 < slot < early:
            vel_load(slot).wait()
        if slot == early:
            wait_whole(vel.at[pl.ds(early, elems - early)], vel_sem.at[early])
        for b in range(half // block):
            if slot == 0:
                wait_whole(vel.at[0, pl.ds(0, 2 * block)], lead_sem.at[b])
            lower = vel[slot, pl.ds(b * block, block), :]
            upper = vel[slot, pl.ds(half + b * block, block), :]
            values = jnp.concatenate([lower, upper], axis=0)
            both = jnp.dot(
                jnp.concatenate(split(values), axis=1), w_slope[...], preferred_element_type=f32
            )
            slope = both[:, :nodes] + both[:, nodes:]
            product = values - dt_step * values * slope
            lower, upper = product[:block], product[block:]
            for parity, value in enumerate((lower + upper, lower - upper)):
                high, low = split(value)
                where = (pl.ds(b * block, block), pl.ds(slot * nodes, nodes))
                folded[(parity, 0) + where] = high
                folded[(parity, 1) + where] = low

    def transform(step, parity, start, stop, at=0, size=rows // 2):
        span = pl.ds(start * nodes, (stop - start) * nodes)
        data_high, data_low = folded[parity, 0, :, span], folded[parity, 1, :, span]
        t_high = table[step, parity, 0, pl.ds(at, size), :]
        t_low = table[step, parity, 1, pl.ds(at, size), :]
        return (
            jnp.dot(t_high, data_high, preferred_element_type=f32)
            + jnp.dot(t_low, data_high, preferred_element_type=f32)
            + jnp.dot(t_high, data_low, preferred_element_type=f32)
        )

    def put_rows(ref, parity, block_rows, start, stop, first_j=0):
        for j in range(block_rows.shape[0] // count):
            for slot in range(start, stop):
                at = (slot - start) * nodes
                ref[parity * per_parity + first_j + j, slot] = block_rows[
                    j * count : (j + 1) * count, at : at + nodes
                ]

    def y_copy(step, k, n):
        start, stop, cuts = spans[k]
        where = (pl.ds(cuts[n], cuts[n + 1] - cuts[n]), pl.ds(start, stop - start))
        return pltpu.make_async_remote_copy(
            sent.at[(step - 1,) + where], rhs.at[(me,) + where],
            y_send.at[step - 1], y_recv.at[step - 1, first_piece[k] + n],
            device_id={"mode": lax.rem(me + step, modes)}, device_id_type=MESH,
        )

    def start_pieces(k, at=0, end=CHUNKS):
        for n, cut in enumerate(spans[k][2][1:]):
            if at < cut <= end:
                for step in range(1, modes):
                    y_copy(step, k, n).start()

    def wait_pieces(late, c, begin=0, end=CHUNKS, also=True):
        for at in range(begin, end):
            due = [
                (k, n)
                for k, (start, _, cuts) in enumerate(spans)
                for n, cut in enumerate(cuts[:-1])
                if cut == at and (start >= early) == late
            ]
            if due:
                @pl.when(jnp.logical_and(c == at, also))
                def _():
                    for k, n in due:
                        for step in range(1, modes):
                            y_copy(step, k, n).wait_recv()

    for k, (start, stop, _) in enumerate(spans):
        for slot in range(start, stop):
            advect(slot)
        if k == 0:
            pl.semaphore_wait(
                barrier, modes - 1 + has_left.astype(jnp.int32) + has_right.astype(jnp.int32)
            )

            each_prev_rim(0, (has_right, "start"), (has_left, "start"))
            each_prev_rim(1, (near_right, "start"), (near_left, "start"))
        for parity in range(2):
            if k == 0:
                for step in range(1, modes):
                    table_load(step, parity).wait()
            cuts = [0, 1, per_parity] if k == 0 and parity == 0 else [0, per_parity]
            for j, stop_j in zip(cuts, cuts[1:]):
                for step in range(1, modes):
                    part = transform(step, parity, start, stop, j * count, (stop_j - j) * count)
                    put_rows(sent.at[step - 1], parity, part, start, stop, j)
                at, end = parity * per_parity + j, parity * per_parity + stop_j
                if start < early:
                    start_pieces(k, at, end)
                else:
                    pl.when(jnp.logical_not(held_back))(lambda: start_pieces(k, at, end))
                if k == 0 and at == REST_AT:
                    start_rest()

    each_prev_rim(1, (far_right, "start"), (far_left, "start"))
    own_table_load.wait()
    for parity in range(2):
        put_rows(rhs.at[me], parity, transform(0, parity, 0, elems), 0, elems)

    wait_whole(taps, small_sem.at[1])
    wait_whole(weights, small_sem.at[2])
    scalar_loads[2].wait()
    set_weights(w_apply, 0, taps[0])
    for f in range(faces):
        matrix = taps[f + 1] + taps[f + 2] if f == faces - 1 and faces < 4 else taps[f + 1]
        set_weights(w_apply, 2 * nodes * (f + 1), matrix)
    eye = lax.broadcasted_iota(jnp.int32, (nodes, nodes), 0) == lax.broadcasted_iota(
        jnp.int32, (nodes, nodes), 1
    )
    diagonal = jnp.sum(jnp.where(eye, taps[0], 0.0), axis=0, keepdims=True)
    pairs[zero_slot] = jnp.zeros((count, 2 * nodes), bf16)
    wait_whole(prev, small_sem.at[4])

    def put_pair(slot, value):
        high, low = split(value)
        pairs[slot, :, pl.ds(0, nodes)] = high
        pairs[slot, :, pl.ds(nodes, nodes)] = low

    def put_halo(halo, c):
        @pl.when(has_left)
        def _():
            for i in range(rim):
                put_pair(i, halo(0, c, i))

        @pl.when(has_right)
        def _():
            for i in range(rim):
                put_pair(rim + group_elems + i, halo(1, c, i))

    def apply():
        columns = [
            jnp.concatenate([pairs[rim + e] for e in range(group_elems)], axis=0)
        ]
        for f in range(faces):
            found = []
            for e in range(group_elems):
                n = near[f, e]
                slot = jnp.clip(n - group * group_elems + rim, 0, zero_slot - 1)
                slot = jnp.where(n >= 0, slot, zero_slot)
                found.append(pairs[slot])
            columns.append(jnp.concatenate(found, axis=0))
        both = jnp.dot(
            jnp.concatenate(columns, axis=1), w_apply[...], preferred_element_type=f32
        )
        return both[:, :nodes] + both[:, nodes:]

    def prev_rows(c, e):
        return prev[c // per_parity, e, pl.ds((c % per_parity) * count, count), :]

    def prev_halo_rows(side, c, i):
        return halo_prev[side, c // per_parity, i, pl.ds((c % per_parity) * count, count), :]

    def shifts(c):
        places = lax.broadcasted_iota(jnp.int32, (count, nodes), 0)
        row = me * rows + 2 * ((c % per_parity) * count + places) + c // per_parity
        wave = jnp.where(row <= half, row, row - half).astype(f32)
        return 4.0 * (wave / half) ** 2

    def complete(c, mode, slot, e):
        first[c, e] = first[c, e] + first_weight * inverse[c, e] * rhs[mode, c, slot]

    def first_sweep(c, carry):
        for e in range(group_elems):
            put_pair(rim + e, prev_rows(c, e))
        for parity in range(2):
            pl.when(c == parity * per_parity)(
                lambda: wait_prev_rims(parity)
            )
        put_halo(prev_halo_rows, c)
        applied = apply()
        shift = shifts(c)
        for e in range(group_elems):
            scaling = weights[0, e] + shift * weights[1, e]
            recip = 1.0 / (diagonal + scaling)
            inverse[c, e] = recip
            value = prev_rows(c, e)
            part = applied[e * count : (e + 1) * count]
            first[c, e] = value - first_weight * recip * (part + scaling * value)
        for slot in range(elems):
            complete(c, me, slot, element_of(me, slot))
        right, left = first_copies(c)
        pl.when(jnp.logical_and(has_right, right_local))(right.start)
        pl.when(jnp.logical_and(has_left, left_local))(left.start)
        return carry

    def finish_rims(c, carry):
        wait_pieces(False, c, 0, per_parity)
        wait_pieces(False, c, per_parity, CHUNKS, jnp.logical_not(held_back))
        for step in range(1, modes):
            mode = lax.rem(me + step, modes)
            for slot in range(early):
                complete(c, mode, slot, element_of(mode, slot))
        right, left = first_copies(c)
        pl.when(jnp.logical_and(has_right, jnp.logical_not(right_local)))(right.start)
        pl.when(jnp.logical_and(has_left, jnp.logical_not(left_local)))(left.start)
        return carry

    def first_half(parity, carry):
        at = parity * per_parity
        lax.fori_loop(at, at + per_parity, first_sweep, 0)
        lax.fori_loop(at, at + per_parity, finish_rims, 0)

        @pl.when(jnp.logical_and(held_back, parity == 0))
        def _():
            wait_pieces(False, per_parity)
            if early < elems:
                start_pieces(len(spans) - 1)

        return carry

    def second_sweep(c, carry):
        for mode in range(modes):
            for slot in range(early):
                e = element_of(mode, slot)
                put_pair(rim + e, first[c, e])
        for slot in range(early, elems):
            e = element_of(me, slot)
            put_pair(rim + e, first[c, e])
        wait_halo_recv(first_copies(c))
        put_halo(lambda side, c, i: halo_first[side, c, i], c)
        if early < elems:
            wait_pieces(True, c)
            for step in range(1, modes):
                mode = lax.rem(me + step, modes)
                for slot in range(early, elems):
                    e = element_of(mode, slot)
                    complete(c, mode, slot, e)
                    put_pair(rim + e, first[c, e])
        applied = apply()
        shift = shifts(c)
        for e in range(group_elems):
            mode, slot = slot_of(e)
            scaling = weights[0, e] + shift * weights[1, e]
            value = first[c, e]
            part = applied[e * count : (e + 1) * count]
            start = (2 * (c % per_parity) * count + c // per_parity) * group_elems + e
            outv[pl.ds(start, count, stride=2 * group_elems), :] = value + second_weight * inverse[
                c, e
            ] * (rhs[mode, c, slot] - (part + scaling * value))
        return carry

    lax.fori_loop(0, 2, first_half, 0)
    lax.fori_loop(0, CHUNKS, second_sweep, 0)

    for side, has in enumerate((has_right, has_left)):
        pl.when(has)(lambda: wait_whole(halo_prev.at[side], p_send.at[side]))
        pl.when(has)(lambda: wait_whole(halo_first.at[side], f_send.at[side]))
    for step in range(1, modes):
        wait_whole(sent.at[step - 1], y_send.at[step - 1])


def faces_of(group_elems):
    return 3 if group_elems // 4 == 2 else 4


def body(modes, groups, velocity, previous, derivative, stiffness, coupling, reaction, axial_weight, neighbours):
    planes, elems, nodes = velocity.shape
    rows, group_elems, _ = previous.shape
    half = planes // 2
    rim = group_elems // 4
    count = rows // CHUNKS
    tables = jnp.asarray(dft_tables(planes, modes))
    run = functools.partial(kernel, modes, groups, planes, elems, group_elems, rows, nodes)
    anywhere = pl.BlockSpec(memory_space=pltpu.HBM)
    dma = pltpu.SemaphoreType.DMA
    taps = faces_of(group_elems) + 1
    scratch = [
        pltpu.VMEM((elems, planes, nodes), f32),
        pltpu.VMEM((2, group_elems, rows // 2, nodes), f32),
        pltpu.VMEM(tables.shape, bf16),
        pltpu.VMEM((nodes, nodes), f32),
        pltpu.VMEM((5, nodes, nodes), f32),
        pltpu.VMEM((2 * nodes, 2 * nodes), bf16),
        pltpu.VMEM((taps * 2 * nodes, 2 * nodes), bf16),
        pltpu.VMEM((2, 2, half, elems * nodes), bf16),
        pltpu.VMEM((modes - 1, CHUNKS, elems, count, nodes), f32),
        pltpu.VMEM((modes, CHUNKS, elems, count, nodes), f32),
        pltpu.VMEM((CHUNKS, group_elems, count, nodes), f32),
        pltpu.VMEM((CHUNKS, group_elems, count, nodes), f32),
        pltpu.VMEM((2, 2, rim, rows // 2, nodes), f32),
        pltpu.VMEM((2, CHUNKS, rim, count, nodes), f32),
        pltpu.VMEM((group_elems + 2 * rim + 1, count, 2 * nodes), bf16),
        pltpu.SMEM((2, group_elems), f32),
        pltpu.SMEM((4, group_elems), jnp.int32),
    ]
    semaphores = [
        dma((half // min(256, half),)),
        dma((min(rim, elems) + 1,)),
        dma((2 * modes - 1,)),
        dma((5,)),
        dma((modes - 1,)),
        dma((modes - 1, PIECES)),
        dma((2,)),
        dma((2, 2)),
        dma((2,)),
        dma((2, CHUNKS)),
    ]
    out = pl.pallas_call(
        run,
        out_shape=pltpu.VMEM((rows * group_elems, nodes), f32),
        in_specs=[anywhere] * 9,
        out_specs=pl.BlockSpec(memory_space=pltpu.VMEM),
        scratch_shapes=scratch + semaphores,
        compiler_params=pltpu.CompilerParams(
            collective_id=0, has_side_effects=True, vmem_limit_bytes=vmem_bytes - 4 * rows * group_elems * nodes - vmem_spare
        ),
        name="advect_helmholtz",
    )(
        velocity,
        previous.reshape(rows // 2, 2, group_elems, nodes),
        tables,
        derivative,
        stiffness,
        coupling,
        reaction,
        axial_weight,
        neighbours.T,
    )
    return out.reshape(rows, group_elems, nodes)


def solution(mesh):
    return jax.shard_map(
        functools.partial(body, mesh.shape["mode"], mesh.shape["elem"]),
        mesh=mesh,
        in_specs=(
            P(None, ("elem", "mode"), None),
            P("mode", "elem", None),
            P(),
            P(),
            P(),
            P("elem"),
            P("elem"),
            P("elem", None),
        ),
        out_specs=P("mode", "elem", None),
        check_vma=False,
    )
```

```python
import functools
import math

import jax
import jax.numpy as jnp
import ml_dtypes
import numpy as np
from jax import lax
from jax.experimental import pallas as pl
from jax.experimental.pallas import tpu as pltpu
from jax.sharding import PartitionSpec as P

dt_step = 0.5
first_weight = 0.7
second_weight = 1.1
CHUNKS = 8
LEAD_CUTS = (0, 1, 4, 8)
EARLY_CUTS = (0, 4, 8)
REST_AT = 0
LATE_CUTS = (0, 2, 4, 6, 7, 8)
PIECES = 10
vmem_bytes = 67043328
vmem_spare = 262144
MESH = pl.DeviceIdType.MESH
bf16 = jnp.bfloat16
f32 = jnp.float32


def dft_tables(planes, modes):
    half = planes // 2
    rows = np.arange(planes)
    waves = np.where(rows <= half, rows, rows - half)
    phase = (waves[:, None] * np.arange(half)[None, :]) % planes
    angles = 2.0 * math.pi / planes * phase
    table = np.where((rows <= half)[:, None], np.cos(angles), -np.sin(angles)) * planes ** (-0.5)
    table = table.reshape(modes, planes // modes // 2, 2, half).transpose(0, 2, 1, 3)
    high = table.astype(ml_dtypes.bfloat16)
    low = (table - high.astype(np.float64)).astype(ml_dtypes.bfloat16)
    return np.stack([high, low], axis=2)


def split(values):
    high = values.astype(bf16)
    low = (values - high.astype(f32)).astype(bf16)
    return high, low


def kernel(
    modes, groups, planes, elems, group_elems, rows, nodes,
    vel_hbm, prev_hbm, table_hbm, der_hbm, stiff_hbm, coup_hbm, reac_hbm, axial_hbm, near_hbm,
    outv,
    vel, prev, table, der, taps, w_slope, w_apply, folded, sent, rhs, first, inverse,
    halo_prev, halo_first, pairs, weights, near,
    lead_sem, vel_sem, table_sem, small_sem, y_send, y_recv, p_send, p_recv, f_send, f_recv,
):
    half = planes // 2
    rim = group_elems // 4
    count = rows // CHUNKS
    per_parity = CHUNKS // 2
    early = min(rim, elems)
    spans = [
        (start, stop, cuts)
        for start, stop, cuts in [
            (0, 1, LEAD_CUTS), (1, early, EARLY_CUTS), (early, elems, LATE_CUTS)
        ]
        if start < stop
    ]
    first_piece = [sum(len(cuts) - 1 for _, _, cuts in spans[:k]) for k in range(len(spans) + 1)]
    faces = faces_of(group_elems)
    me = lax.axis_index("mode")
    group = lax.axis_index("elem")
    zero_slot = group_elems + 2 * rim

    def skip(mode):
        return jnp.where(mode < modes // 2, 0, elems - early)

    def element_of(mode, slot):
        if isinstance(mode, int):
            turn = 0 if mode < modes // 2 else elems - early
            return mode * elems + (slot + turn) % elems
        return mode * elems + lax.rem(slot + skip(mode), elems)

    def slot_of(element):
        mode, place = element // elems, element % elems
        turn = 0 if mode < modes // 2 else elems - early
        return mode, (place - turn) % elems

    der_load = pltpu.make_async_copy(der_hbm, der, small_sem.at[0])
    stiff_load = pltpu.make_async_copy(stiff_hbm, taps.at[0], small_sem.at[1])
    coup_load = pltpu.make_async_copy(coup_hbm, taps.at[pl.ds(1, 4)], small_sem.at[1])

    scalar_loads = [
        pltpu.make_async_copy(src, dst, small_sem.at[i])
        for i, src, dst in [
            (2, reac_hbm, weights.at[0]), (2, axial_hbm, weights.at[1]), (3, near_hbm, near)
        ]
    ]

    block = min(256, half)

    def vel_load(slot):
        return pltpu.make_async_copy(
            vel_hbm.at[:, lax.rem(slot + skip(me), elems)], vel.at[slot], vel_sem.at[min(slot, early)]
        )

    def lead_load(b, side):
        where = pl.ds(side * half + b * block, block)
        return pltpu.make_async_copy(
            vel_hbm.at[where, skip(me)], vel.at[0, where], lead_sem.at[b]
        )

    def wait_whole(ref, sem):
        pltpu.make_async_copy(ref, ref, sem).wait()

    def table_load(step, parity):
        owner = lax.rem(me + step, modes)
        return pltpu.make_async_copy(
            table_hbm.at[owner, parity], table.at[step, parity], table_sem.at[2 * step - 1 + parity]
        )

    own_table_load = pltpu.make_async_copy(table_hbm.at[me], table.at[0], table_sem.at[0])

    def prev_load(parity, e):
        return pltpu.make_async_copy(
            prev_hbm.at[:, parity, e], prev.at[parity, e], small_sem.at[4]
        )

    steps = [*range(1, modes), 0]
    der_load.start()
    for b in range(half // block):
        for side in range(2):
            lead_load(b, side).start()
    for step in range(1, modes):
        table_load(step, 0).start()
    def start_rest():
        for slot in range(early, elems):
            vel_load(slot).start()
        own_table_load.start()
        for parity in range(2):
            for e in range(group_elems):
                prev_load(parity, e).start()
        stiff_load.start()
        coup_load.start()
        for load in scalar_loads:
            load.start()

    barrier = pltpu.get_barrier_semaphore()
    for step in range(1, modes):
        pl.semaphore_signal(
            barrier, inc=1, device_id={"mode": lax.rem(me + step, modes)}, device_id_type=MESH
        )
    has_left = group > 0
    has_right = group < groups - 1

    @pl.when(has_left)
    def _():
        pl.semaphore_signal(barrier, inc=1, device_id={"elem": group - 1}, device_id_type=MESH)

    @pl.when(has_right)
    def _():
        pl.semaphore_signal(barrier, inc=1, device_id={"elem": group + 1}, device_id_type=MESH)

    def halo_copies(source, halo, send, recv, c):
        right = pltpu.make_async_remote_copy(
            source(c, 0), halo.at[0, c], send.at[0], recv.at[0, c],
            device_id={"elem": group + 1}, device_id_type=MESH,
        )
        left = pltpu.make_async_remote_copy(
            source(c, 1), halo.at[1, c], send.at[1], recv.at[1, c],
            device_id={"elem": group - 1}, device_id_type=MESH,
        )
        return right, left

    def prev_rim(parity, side, i):
        return pltpu.make_async_remote_copy(
            prev_hbm.at[:, parity, (group_elems - rim) * (1 - side) + i],
            halo_prev.at[side, parity, i], p_send.at[side], p_recv.at[side, parity],
            device_id={"elem": group + 1 - 2 * side}, device_id_type=MESH,
        )

    def wait_prev_rims(parity):
        pl.when(has_left)(lambda: wait_whole(halo_prev.at[0, parity], p_recv.at[0, parity]))
        pl.when(has_right)(lambda: wait_whole(halo_prev.at[1, parity], p_recv.at[1, parity]))

    def first_copies(c):
        def source(c, side):
            return first.at[c, pl.ds((group_elems - rim) * (1 - side), rim)]

        return halo_copies(source, halo_first, f_send, f_recv, c)

    def wait_halo_recv(copies):
        right, left = copies
        pl.when(has_left)(right.wait_recv)
        pl.when(has_right)(left.wait_recv)

    def each_prev_rim(parity, act_right, act_left):
        for i in range(rim):
            right, left = prev_rim(parity, 0, i), prev_rim(parity, 1, i)
            pl.when(act_right[0])(getattr(right, act_right[1]))
            pl.when(act_left[0])(getattr(left, act_left[1]))

    far_right = jnp.logical_and(has_right, lax.rem(group, 4) == 3)
    far_left = jnp.logical_and(has_left, lax.rem(group, 4) == 0)
    near_right = jnp.logical_and(has_right, lax.rem(group, 4) != 3)
    near_left = jnp.logical_and(has_left, lax.rem(group, 4) != 0)
    left_local = me == 0
    right_local = jnp.logical_and(me == modes - 1, lax.rem(group, 4) != 3)
    held_back = lax.rem(group, 2) == 1

    def set_weights(ref, at, matrix):
        high, low = split(matrix.T)
        for part in range(2):
            ref[pl.ds(at + part * nodes, nodes), pl.ds(0, nodes)] = high
            ref[pl.ds(at + part * nodes, nodes), pl.ds(nodes, nodes)] = low

    der_load.wait()
    for slot in range(1, early):
        vel_load(slot).start()
    for step in range(1, modes):
        table_load(step, 1).start()
    set_weights(w_slope, 0, der[...])

    def advect(slot):
        if 0 < slot < early:
            vel_load(slot).wait()
        if slot == early:
            wait_whole(vel.at[pl.ds(early, elems - early)], vel_sem.at[early])
        for b in range(half // block):
            if slot == 0:
                wait_whole(vel.at[0, pl.ds(0, 2 * block)], lead_sem.at[b])
            lower = vel[slot, pl.ds(b * block, block), :]
            upper = vel[slot, pl.ds(half + b * block, block), :]
            values = jnp.concatenate([lower, upper], axis=0)
            both = jnp.dot(
                jnp.concatenate(split(values), axis=1), w_slope[...], preferred_element_type=f32
            )
            slope = both[:, :nodes] + both[:, nodes:]
            product = values - dt_step * values * slope
            lower, upper = product[:block], product[block:]
            for parity, value in enumerate((lower + upper, lower - upper)):
                high, low = split(value)
                where = (pl.ds(b * block, block), pl.ds(slot * nodes, nodes))
                folded[(parity, 0) + where] = high
                folded[(parity, 1) + where] = low

    def transform(step, parity, start, stop, at=0, size=rows // 2):
        span = pl.ds(start * nodes, (stop - start) * nodes)
        data_high, data_low = folded[parity, 0, :, span], folded[parity, 1, :, span]
        t_high = table[step, parity, 0, pl.ds(at, size), :]
        t_low = table[step, parity, 1, pl.ds(at, size), :]
        return (
            jnp.dot(t_high, data_high, preferred_element_type=f32)
            + jnp.dot(t_low, data_high, preferred_element_type=f32)
            + jnp.dot(t_high, data_low, preferred_element_type=f32)
        )

    def put_rows(ref, parity, block_rows, start, stop, first_j=0):
        for j in range(block_rows.shape[0] // count):
            for slot in range(start, stop):
                at = (slot - start) * nodes
                ref[parity * per_parity + first_j + j, slot] = block_rows[
                    j * count : (j + 1) * count, at : at + nodes
                ]

    def y_copy(step, k, n):
        start, stop, cuts = spans[k]
        where = (pl.ds(cuts[n], cuts[n + 1] - cuts[n]), pl.ds(start, stop - start))
        return pltpu.make_async_remote_copy(
            sent.at[(step - 1,) + where], rhs.at[(me,) + where],
            y_send.at[step - 1], y_recv.at[step - 1, first_piece[k] + n],
            device_id={"mode": lax.rem(me + step, modes)}, device_id_type=MESH,
        )

    def start_pieces(k, at=0, end=CHUNKS):
        for n, cut in enumerate(spans[k][2][1:]):
            if at < cut <= end:
                for step in range(1, modes):
                    y_copy(step, k, n).start()

    def wait_pieces(late, c, begin=0, end=CHUNKS, also=True):
        for at in range(begin, end):
            due = [
                (k, n)
                for k, (start, _, cuts) in enumerate(spans)
                for n, cut in enumerate(cuts[:-1])
                if cut == at and (start >= early) == late
            ]
            if due:
                @pl.when(jnp.logical_and(c == at, also))
                def _():
                    for k, n in due:
                        for step in range(1, modes):
                            y_copy(step, k, n).wait_recv()

    for k, (start, stop, _) in enumerate(spans):
        for slot in range(start, stop):
            advect(slot)
        if k == 0:
            pl.semaphore_wait(
                barrier, modes - 1 + has_left.astype(jnp.int32) + has_right.astype(jnp.int32)
            )

            each_prev_rim(0, (has_right, "start"), (has_left, "start"))
            each_prev_rim(1, (near_right, "start"), (near_left, "start"))
        for parity in range(2):
            if k == 0:
                for step in range(1, modes):
                    table_load(step, parity).wait()
            cuts = [0, 1, per_parity] if k == 0 and parity == 0 else [0, per_parity]
            for j, stop_j in zip(cuts, cuts[1:]):
                for step in range(1, modes):
                    part = transform(step, parity, start, stop, j * count, (stop_j - j) * count)
                    put_rows(sent.at[step - 1], parity, part, start, stop, j)
                at, end = parity * per_parity + j, parity * per_parity + stop_j
                if start < early:
                    start_pieces(k, at, end)
                else:
                    pl.when(jnp.logical_not(held_back))(lambda: start_pieces(k, at, end))
                if k == 0 and at == REST_AT:
                    start_rest()

    each_prev_rim(1, (far_right, "start"), (far_left, "start"))
    own_table_load.wait()
    for parity in range(2):
        put_rows(rhs.at[me], parity, transform(0, parity, 0, elems), 0, elems)

    wait_whole(taps, small_sem.at[1])
    wait_whole(weights, small_sem.at[2])
    scalar_loads[2].wait()
    set_weights(w_apply, 0, taps[0])
    for f in range(faces):
        matrix = taps[f + 1] + taps[f + 2] if f == faces - 1 and faces < 4 else taps[f + 1]
        set_weights(w_apply, 2 * nodes * (f + 1), matrix)
    eye = lax.broadcasted_iota(jnp.int32, (nodes, nodes), 0) == lax.broadcasted_iota(
        jnp.int32, (nodes, nodes), 1
    )
    diagonal = jnp.sum(jnp.where(eye, taps[0], 0.0), axis=0, keepdims=True)
    pairs[zero_slot] = jnp.zeros((count, 2 * nodes), bf16)
    wait_whole(prev, small_sem.at[4])

    def put_pair(slot, value):
        high, low = split(value)
        pairs[slot, :, pl.ds(0, nodes)] = high
        pairs[slot, :, pl.ds(nodes, nodes)] = low

    def put_halo(halo, c):
        @pl.when(has_left)
        def _():
            for i in range(rim):
                put_pair(i, halo(0, c, i))

        @pl.when(has_right)
        def _():
            for i in range(rim):
                put_pair(rim + group_elems + i, halo(1, c, i))

    def apply():
        columns = [
            jnp.concatenate([pairs[rim + e] for e in range(group_elems)], axis=0)
        ]
        for f in range(faces):
            found = []
            for e in range(group_elems):
                n = near[f, e]
                slot = jnp.clip(n - group * group_elems + rim, 0, zero_slot - 1)
                slot = jnp.where(n >= 0, slot, zero_slot)
                found.append(pairs[slot])
            columns.append(jnp.concatenate(found, axis=0))
        both = jnp.dot(
            jnp.concatenate(columns, axis=1), w_apply[...], preferred_element_type=f32
        )
        return both[:, :nodes] + both[:, nodes:]

    def prev_rows(c, e):
        return prev[c // per_parity, e, pl.ds((c % per_parity) * count, count), :]

    def prev_halo_rows(side, c, i):
        return halo_prev[side, c // per_parity, i, pl.ds((c % per_parity) * count, count), :]

    def shifts(c):
        places = lax.broadcasted_iota(jnp.int32, (count, nodes), 0)
        row = me * rows + 2 * ((c % per_parity) * count + places) + c // per_parity
        wave = jnp.where(row <= half, row, row - half).astype(f32)
        return 4.0 * (wave / half) ** 2

    def complete(c, mode, slot, e):
        first[c, e] = first[c, e] + first_weight * inverse[c, e] * rhs[mode, c, slot]

    def first_sweep(c, carry):
        for e in range(group_elems):
            put_pair(rim + e, prev_rows(c, e))
        for parity in range(2):
            pl.when(c == parity * per_parity)(
                lambda: wait_prev_rims(parity)
            )
        put_halo(prev_halo_rows, c)
        applied = apply()
        shift = shifts(c)
        for e in range(group_elems):
            scaling = weights[0, e] + shift * weights[1, e]
            recip = 1.0 / (diagonal + scaling)
            inverse[c, e] = recip
            value = prev_rows(c, e)
            part = applied[e * count : (e + 1) * count]
            first[c, e] = value - first_weight * recip * (part + scaling * value)
        for slot in range(elems):
            complete(c, me, slot, element_of(me, slot))
        right, left = first_copies(c)
        pl.when(jnp.logical_and(has_right, right_local))(right.start)
        pl.when(jnp.logical_and(has_left, left_local))(left.start)
        return carry

    def finish_rims(c, carry):
        wait_pieces(False, c, 0, per_parity)
        wait_pieces(False, c, per_parity, CHUNKS, jnp.logical_not(held_back))
        for step in range(1, modes):
            mode = lax.rem(me + step, modes)
            for slot in range(early):
                complete(c, mode, slot, element_of(mode, slot))
        right, left = first_copies(c)
        pl.when(jnp.logical_and(has_right, jnp.logical_not(right_local)))(right.start)
        pl.when(jnp.logical_and(has_left, jnp.logical_not(left_local)))(left.start)
        return carry

    def first_half(parity, carry):
        at = parity * per_parity
        lax.fori_loop(at, at + per_parity, first_sweep, 0)
        lax.fori_loop(at, at + per_parity, finish_rims, 0)

        @pl.when(jnp.logical_and(held_back, parity == 0))
        def _():
            wait_pieces(False, per_parity)
            if early < elems:
                start_pieces(len(spans) - 1)

        return carry

    def second_sweep(c, carry):
        for mode in range(modes):
            for slot in range(early):
                e = element_of(mode, slot)
                put_pair(rim + e, first[c, e])
        for slot in range(early, elems):
            e = element_of(me, slot)
            put_pair(rim + e, first[c, e])
        wait_halo_recv(first_copies(c))
        put_halo(lambda side, c, i: halo_first[side, c, i], c)
        if early < elems:
            wait_pieces(True, c)
            for step in range(1, modes):
                mode = lax.rem(me + step, modes)
                for slot in range(early, elems):
                    e = element_of(mode, slot)
                    complete(c, mode, slot, e)
                    put_pair(rim + e, first[c, e])
        applied = apply()
        shift = shifts(c)
        for e in range(group_elems):
            mode, slot = slot_of(e)
            scaling = weights[0, e] + shift * weights[1, e]
            value = first[c, e]
            part = applied[e * count : (e + 1) * count]
            start = (2 * (c % per_parity) * count + c // per_parity) * group_elems + e
            outv[pl.ds(start, count, stride=2 * group_elems), :] = value + second_weight * inverse[
                c, e
            ] * (rhs[mode, c, slot] - (part + scaling * value))
        return carry

    lax.fori_loop(0, 2, first_half, 0)
    lax.fori_loop(0, CHUNKS, second_sweep, 0)

    for side, has in enumerate((has_right, has_left)):
        pl.when(has)(lambda: wait_whole(halo_prev.at[side], p_send.at[side]))
        pl.when(has)(lambda: wait_whole(halo_first.at[side], f_send.at[side]))
    for step in range(1, modes):
        wait_whole(sent.at[step - 1], y_send.at[step - 1])


def faces_of(group_elems):
    return 3 if group_elems // 4 == 2 else 4


def body(modes, groups, velocity, previous, derivative, stiffness, coupling, reaction, axial_weight, neighbours):
    planes, elems, nodes = velocity.shape
    rows, group_elems, _ = previous.shape
    half = planes // 2
    rim = group_elems // 4
    count = rows // CHUNKS
    tables = jnp.asarray(dft_tables(planes, modes))
    run = functools.partial(kernel, modes, groups, planes, elems, group_elems, rows, nodes)
    anywhere = pl.BlockSpec(memory_space=pltpu.HBM)
    dma = pltpu.SemaphoreType.DMA
    taps = faces_of(group_elems) + 1
    scratch = [
        pltpu.VMEM((elems, planes, nodes), f32),
        pltpu.VMEM((2, group_elems, rows // 2, nodes), f32),
        pltpu.VMEM(tables.shape, bf16),
        pltpu.VMEM((nodes, nodes), f32),
        pltpu.VMEM((5, nodes, nodes), f32),
        pltpu.VMEM((2 * nodes, 2 * nodes), bf16),
        pltpu.VMEM((taps * 2 * nodes, 2 * nodes), bf16),
        pltpu.VMEM((2, 2, half, elems * nodes), bf16),
        pltpu.VMEM((modes - 1, CHUNKS, elems, count, nodes), f32),
        pltpu.VMEM((modes, CHUNKS, elems, count, nodes), f32),
        pltpu.VMEM((CHUNKS, group_elems, count, nodes), f32),
        pltpu.VMEM((CHUNKS, group_elems, count, nodes), f32),
        pltpu.VMEM((2, 2, rim, rows // 2, nodes), f32),
        pltpu.VMEM((2, CHUNKS, rim, count, nodes), f32),
        pltpu.VMEM((group_elems + 2 * rim + 1, count, 2 * nodes), bf16),
        pltpu.SMEM((2, group_elems), f32),
        pltpu.SMEM((4, group_elems), jnp.int32),
    ]
    semaphores = [
        dma((half // min(256, half),)),
        dma((min(rim, elems) + 1,)),
        dma((2 * modes - 1,)),
        dma((5,)),
        dma((modes - 1,)),
        dma((modes - 1, PIECES)),
        dma((2,)),
        dma((2, 2)),
        dma((2,)),
        dma((2, CHUNKS)),
    ]
    out = pl.pallas_call(
        run,
        out_shape=pltpu.VMEM((rows * group_elems, nodes), f32),
        in_specs=[anywhere] * 9,
        out_specs=pl.BlockSpec(memory_space=pltpu.VMEM),
        scratch_shapes=scratch + semaphores,
        compiler_params=pltpu.CompilerParams(
            collective_id=0, has_side_effects=True, vmem_limit_bytes=vmem_bytes - 4 * rows * group_elems * nodes - vmem_spare
        ),
        name="advect_helmholtz",
    )(
        velocity,
        previous.reshape(rows // 2, 2, group_elems, nodes),
        tables,
        derivative,
        stiffness,
        coupling,
        reaction,
        axial_weight,
        neighbours.T,
    )
    return out.reshape(rows, group_elems, nodes)


def solution(mesh):
    return jax.shard_map(
        functools.partial(body, mesh.shape["mode"], mesh.shape["elem"]),
        mesh=mesh,
        in_specs=(
            P(None, ("elem", "mode"), None),
            P("mode", "elem", None),
            P(),
            P(),
            P(),
            P("elem"),
            P("elem"),
            P("elem", None),
        ),
        out_specs=P("mode", "elem", None),
        check_vma=False,
    )
```

```python
import functools
import math

import jax
import jax.numpy as jnp
import ml_dtypes
import numpy as np
from jax import lax
from jax.experimental import pallas as pl
from jax.experimental.pallas import tpu as pltpu
from jax.sharding import PartitionSpec as P

dt_step = 0.5
first_weight = 0.7
second_weight = 1.1
CHUNKS = 8
LEAD_CUTS = (0, 1, 4, 8)
EARLY_CUTS = (0, 4, 8)
REST_AT = 0
LATE_CUTS = (0, 2, 4, 6, 7, 8)
PIECES = 7
vmem_bytes = 67043328
vmem_spare = 262144
MESH = pl.DeviceIdType.MESH
bf16 = jnp.bfloat16
f32 = jnp.float32


def dft_tables(planes, modes):
    half = planes // 2
    rows = np.arange(planes)
    waves = np.where(rows <= half, rows, rows - half)
    phase = (waves[:, None] * np.arange(half)[None, :]) % planes
    angles = 2.0 * math.pi / planes * phase
    table = np.where((rows <= half)[:, None], np.cos(angles), -np.sin(angles)) * planes ** (-0.5)
    table = table.reshape(modes, planes // modes // 2, 2, half).transpose(0, 2, 1, 3)
    high = table.astype(ml_dtypes.bfloat16)
    low = (table - high.astype(np.float64)).astype(ml_dtypes.bfloat16)
    return np.stack([high, low], axis=2)


def split(values):
    high = values.astype(bf16)
    low = (values - high.astype(f32)).astype(bf16)
    return high, low


def kernel(
    modes, groups, planes, elems, group_elems, rows, nodes,
    vel_hbm, prev_hbm, table_hbm, der_hbm, stiff_hbm, coup_hbm, reac_hbm, axial_hbm, near_hbm,
    outv,
    vel, prev, table, der, taps, w_slope, w_apply, folded, sent, rhs, first, inverse,
    halo_prev, halo_first, pairs, weights, near,
    lead_sem, vel_sem, table_sem, small_sem, y_send, y_recv, p_send, p_recv, f_send, f_recv,
):
    half = planes // 2
    rim = group_elems // 4
    count = rows // CHUNKS
    per_parity = CHUNKS // 2
    early = min(rim, elems)
    spans = [
        (start, stop, cuts)
        for start, stop, cuts in [
            (0, 1, LEAD_CUTS), (1, early, EARLY_CUTS), (early, elems, LATE_CUTS)
        ]
        if start < stop
    ]
    faces = faces_of(group_elems)
    me = lax.axis_index("mode")
    group = lax.axis_index("elem")
    zero_slot = group_elems + 2 * rim

    def skip(mode):
        return jnp.where(mode < modes // 2, 0, elems - early)

    def element_of(mode, slot):
        if isinstance(mode, int):
            turn = 0 if mode < modes // 2 else elems - early
            return mode * elems + (slot + turn) % elems
        return mode * elems + lax.rem(slot + skip(mode), elems)

    def slot_of(element):
        mode, place = element // elems, element % elems
        turn = 0 if mode < modes // 2 else elems - early
        return mode, (place - turn) % elems

    der_load = pltpu.make_async_copy(der_hbm, der, small_sem.at[0])
    stiff_load = pltpu.make_async_copy(stiff_hbm, taps.at[0], small_sem.at[1])
    coup_load = pltpu.make_async_copy(coup_hbm, taps.at[pl.ds(1, 4)], small_sem.at[1])

    scalar_loads = [
        pltpu.make_async_copy(src, dst, small_sem.at[i])
        for i, src, dst in [
            (2, reac_hbm, weights.at[0]), (2, axial_hbm, weights.at[1]), (3, near_hbm, near)
        ]
    ]

    block = min(256, half)

    def vel_load(slot):
        return pltpu.make_async_copy(
            vel_hbm.at[:, lax.rem(slot + skip(me), elems)], vel.at[slot], vel_sem.at[min(slot, early)]
        )

    def lead_load(b, side):
        where = pl.ds(side * half + b * block, block)
        return pltpu.make_async_copy(
            vel_hbm.at[where, skip(me)], vel.at[0, where], lead_sem.at[b]
        )

    def wait_whole(ref, sem):
        pltpu.make_async_copy(ref, ref, sem).wait()

    def table_load(step, parity):
        owner = lax.rem(me + step, modes)
        return pltpu.make_async_copy(
            table_hbm.at[owner, parity], table.at[step, parity], table_sem.at[2 * step - 1 + parity]
        )

    own_table_load = pltpu.make_async_copy(table_hbm.at[me], table.at[0], table_sem.at[0])

    def prev_load(parity, e):
        return pltpu.make_async_copy(
            prev_hbm.at[:, parity, e], prev.at[parity, e], small_sem.at[4]
        )

    steps = [*range(1, modes), 0]
    der_load.start()
    for b in range(half // block):
        for side in range(2):
            lead_load(b, side).start()
    for step in range(1, modes):
        table_load(step, 0).start()
    def start_rest():
        for slot in range(early, elems):
            vel_load(slot).start()
        own_table_load.start()
        for parity in range(2):
            for e in range(group_elems):
                prev_load(parity, e).start()
        stiff_load.start()
        coup_load.start()
        for load in scalar_loads:
            load.start()

    barrier = pltpu.get_barrier_semaphore()
    for step in range(1, modes):
        pl.semaphore_signal(
            barrier, inc=1, device_id={"mode": lax.rem(me + step, modes)}, device_id_type=MESH
        )
    has_left = group > 0
    has_right = group < groups - 1

    @pl.when(has_left)
    def _():
        pl.semaphore_signal(barrier, inc=1, device_id={"elem": group - 1}, device_id_type=MESH)

    @pl.when(has_right)
    def _():
        pl.semaphore_signal(barrier, inc=1, device_id={"elem": group + 1}, device_id_type=MESH)

    def halo_slot(c):
        return jnp.maximum(c - per_parity + 1, 0)

    def halo_copies(source, halo, send, recv, c):
        right = pltpu.make_async_remote_copy(
            source(c, 0), halo.at[0, c], send.at[0], recv.at[0, halo_slot(c)],
            device_id={"elem": group + 1}, device_id_type=MESH,
        )
        left = pltpu.make_async_remote_copy(
            source(c, 1), halo.at[1, c], send.at[1], recv.at[1, halo_slot(c)],
            device_id={"elem": group - 1}, device_id_type=MESH,
        )
        return right, left

    def prev_rim(parity, side, i):
        return pltpu.make_async_remote_copy(
            prev_hbm.at[:, parity, (group_elems - rim) * (1 - side) + i],
            halo_prev.at[side, parity, i], p_send.at[side], p_recv.at[side, parity],
            device_id={"elem": group + 1 - 2 * side}, device_id_type=MESH,
        )

    def wait_prev_rims(parity):
        pl.when(has_left)(lambda: wait_whole(halo_prev.at[0, parity], p_recv.at[0, parity]))
        pl.when(has_right)(lambda: wait_whole(halo_prev.at[1, parity], p_recv.at[1, parity]))

    def first_copies(c):
        def source(c, side):
            return first.at[c, pl.ds((group_elems - rim) * (1 - side), rim)]

        return halo_copies(source, halo_first, f_send, f_recv, c)

    def wait_halo_recv(copies):
        right, left = copies
        pl.when(has_left)(right.wait_recv)
        pl.when(has_right)(left.wait_recv)

    def each_prev_rim(parity, act_right, act_left):
        for i in range(rim):
            right, left = prev_rim(parity, 0, i), prev_rim(parity, 1, i)
            pl.when(act_right[0])(getattr(right, act_right[1]))
            pl.when(act_left[0])(getattr(left, act_left[1]))

    far_right = jnp.logical_and(has_right, lax.rem(group, 4) == 3)
    far_left = jnp.logical_and(has_left, lax.rem(group, 4) == 0)
    near_right = jnp.logical_and(has_right, lax.rem(group, 4) != 3)
    near_left = jnp.logical_and(has_left, lax.rem(group, 4) != 0)
    left_local = me == 0
    right_local = jnp.logical_and(me == modes - 1, lax.rem(group, 4) != 3)
    held_back = lax.rem(group, 2) == 1

    def set_weights(ref, at, matrix):
        high, low = split(matrix.T)
        for part in range(2):
            ref[pl.ds(at + part * nodes, nodes), pl.ds(0, nodes)] = high
            ref[pl.ds(at + part * nodes, nodes), pl.ds(nodes, nodes)] = low

    der_load.wait()
    for slot in range(1, early):
        vel_load(slot).start()
    for step in range(1, modes):
        table_load(step, 1).start()
    set_weights(w_slope, 0, der[...])

    def advect(slot):
        if 0 < slot < early:
            vel_load(slot).wait()
        if slot == early:
            wait_whole(vel.at[pl.ds(early, elems - early)], vel_sem.at[early])
        for b in range(half // block):
            if slot == 0:
                wait_whole(vel.at[0, pl.ds(0, 2 * block)], lead_sem.at[b])
            lower = vel[slot, pl.ds(b * block, block), :]
            upper = vel[slot, pl.ds(half + b * block, block), :]
            values = jnp.concatenate([lower, upper], axis=0)
            both = jnp.dot(
                jnp.concatenate(split(values), axis=1), w_slope[...], preferred_element_type=f32
            )
            slope = both[:, :nodes] + both[:, nodes:]
            product = values - dt_step * values * slope
            lower, upper = product[:block], product[block:]
            for parity, value in enumerate((lower + upper, lower - upper)):
                high, low = split(value)
                where = (pl.ds(b * block, block), pl.ds(slot * nodes, nodes))
                folded[(parity, 0) + where] = high
                folded[(parity, 1) + where] = low

    def transform(step, parity, start, stop, at=0, size=rows // 2):
        span = pl.ds(start * nodes, (stop - start) * nodes)
        data_high, data_low = folded[parity, 0, :, span], folded[parity, 1, :, span]
        t_high = table[step, parity, 0, pl.ds(at, size), :]
        t_low = table[step, parity, 1, pl.ds(at, size), :]
        return (
            jnp.dot(t_high, data_high, preferred_element_type=f32)
            + jnp.dot(t_low, data_high, preferred_element_type=f32)
            + jnp.dot(t_high, data_low, preferred_element_type=f32)
        )

    def put_rows(ref, parity, block_rows, start, stop, first_j=0):
        for j in range(block_rows.shape[0] // count):
            for slot in range(start, stop):
                at = (slot - start) * nodes
                ref[parity * per_parity + first_j + j, slot] = block_rows[
                    j * count : (j + 1) * count, at : at + nodes
                ]

    def piece_slot(k, n):
        start, _, cuts = spans[k]
        return 2 + n if start >= early else int(cuts[n] >= per_parity)

    def y_copy(step, k, n):
        start, stop, cuts = spans[k]
        where = (pl.ds(cuts[n], cuts[n + 1] - cuts[n]), pl.ds(start, stop - start))
        return pltpu.make_async_remote_copy(
            sent.at[(step - 1,) + where], rhs.at[(me,) + where],
            y_send.at[step - 1], y_recv.at[step - 1, piece_slot(k, n)],
            device_id={"mode": lax.rem(me + step, modes)}, device_id_type=MESH,
        )

    def start_pieces(k, at=0, end=CHUNKS):
        for n, cut in enumerate(spans[k][2][1:]):
            if at < cut <= end:
                for step in range(1, modes):
                    y_copy(step, k, n).start()

    def wait_pieces(late, c, begin=0, end=CHUNKS, also=True):
        for parity in range(2):
            at = parity * per_parity
            if not late and begin <= at < end:
                @pl.when(jnp.logical_and(c == at, also))
                def _():
                    for step in range(1, modes):
                        mode = lax.rem(me + modes - step, modes)
                        whole = rhs.at[mode, pl.ds(at, per_parity), pl.ds(0, early)]
                        wait_whole(whole, y_recv.at[step - 1, parity])

        if not late:
            return
        for at in range(begin, end):
            due = [
                (k, n)
                for k, (start, _, cuts) in enumerate(spans)
                for n, cut in enumerate(cuts[:-1])
                if cut == at and (start >= early) == late
            ]
            if due:
                @pl.when(jnp.logical_and(c == at, also))
                def _():
                    for k, n in due:
                        for step in range(1, modes):
                            y_copy(step, k, n).wait_recv()

    for k, (start, stop, _) in enumerate(spans):
        for slot in range(start, stop):
            advect(slot)
        if k == 0:
            pl.semaphore_wait(
                barrier, modes - 1 + has_left.astype(jnp.int32) + has_right.astype(jnp.int32)
            )

            each_prev_rim(0, (has_right, "start"), (has_left, "start"))
            each_prev_rim(1, (near_right, "start"), (near_left, "start"))
        for parity in range(2):
            if k == 0:
                for step in range(1, modes):
                    table_load(step, parity).wait()
            cuts = [0, 1, per_parity] if k == 0 and parity == 0 else [0, per_parity]
            for j, stop_j in zip(cuts, cuts[1:]):
                for step in range(1, modes):
                    part = transform(step, parity, start, stop, j * count, (stop_j - j) * count)
                    put_rows(sent.at[step - 1], parity, part, start, stop, j)
                at, end = parity * per_parity + j, parity * per_parity + stop_j
                if start < early:
                    start_pieces(k, at, end)
                else:
                    pl.when(jnp.logical_not(held_back))(lambda: start_pieces(k, at, end))
                if k == 0 and at == REST_AT:
                    start_rest()

    each_prev_rim(1, (far_right, "start"), (far_left, "start"))
    own_table_load.wait()
    for parity in range(2):
        put_rows(rhs.at[me], parity, transform(0, parity, 0, elems), 0, elems)

    wait_whole(taps, small_sem.at[1])
    wait_whole(weights, small_sem.at[2])
    scalar_loads[2].wait()
    set_weights(w_apply, 0, taps[0])
    for f in range(faces):
        matrix = taps[f + 1] + taps[f + 2] if f == faces - 1 and faces < 4 else taps[f + 1]
        set_weights(w_apply, 2 * nodes * (f + 1), matrix)
    eye = lax.broadcasted_iota(jnp.int32, (nodes, nodes), 0) == lax.broadcasted_iota(
        jnp.int32, (nodes, nodes), 1
    )
    diagonal = jnp.sum(jnp.where(eye, taps[0], 0.0), axis=0, keepdims=True)
    pairs[zero_slot] = jnp.zeros((count, 2 * nodes), bf16)
    wait_whole(prev, small_sem.at[4])

    def put_pair(slot, value):
        high, low = split(value)
        pairs[slot, :, pl.ds(0, nodes)] = high
        pairs[slot, :, pl.ds(nodes, nodes)] = low

    def put_halo(halo, c):
        @pl.when(has_left)
        def _():
            for i in range(rim):
                put_pair(i, halo(0, c, i))

        @pl.when(has_right)
        def _():
            for i in range(rim):
                put_pair(rim + group_elems + i, halo(1, c, i))

    def apply():
        columns = [
            jnp.concatenate([pairs[rim + e] for e in range(group_elems)], axis=0)
        ]
        for f in range(faces):
            found = []
            for e in range(group_elems):
                n = near[f, e]
                slot = jnp.clip(n - group * group_elems + rim, 0, zero_slot - 1)
                slot = jnp.where(n >= 0, slot, zero_slot)
                found.append(pairs[slot])
            columns.append(jnp.concatenate(found, axis=0))
        both = jnp.dot(
            jnp.concatenate(columns, axis=1), w_apply[...], preferred_element_type=f32
        )
        return both[:, :nodes] + both[:, nodes:]

    def prev_rows(c, e):
        return prev[c // per_parity, e, pl.ds((c % per_parity) * count, count), :]

    def prev_halo_rows(side, c, i):
        return halo_prev[side, c // per_parity, i, pl.ds((c % per_parity) * count, count), :]

    def shifts(c):
        places = lax.broadcasted_iota(jnp.int32, (count, nodes), 0)
        row = me * rows + 2 * ((c % per_parity) * count + places) + c // per_parity
        wave = jnp.where(row <= half, row, row - half).astype(f32)
        return 4.0 * (wave / half) ** 2

    def complete(c, mode, slot, e):
        first[c, e] = first[c, e] + first_weight * inverse[c, e] * rhs[mode, c, slot]

    def first_sweep(c, carry):
        for e in range(group_elems):
            put_pair(rim + e, prev_rows(c, e))
        for parity in range(2):
            pl.when(c == parity * per_parity)(
                lambda: wait_prev_rims(parity)
            )
        put_halo(prev_halo_rows, c)
        applied = apply()
        shift = shifts(c)
        for e in range(group_elems):
            scaling = weights[0, e] + shift * weights[1, e]
            recip = 1.0 / (diagonal + scaling)
            inverse[c, e] = recip
            value = prev_rows(c, e)
            part = applied[e * count : (e + 1) * count]
            first[c, e] = value - first_weight * recip * (part + scaling * value)
        for slot in range(elems):
            complete(c, me, slot, element_of(me, slot))
        right, left = first_copies(c)
        pl.when(jnp.logical_and(has_right, right_local))(right.start)
        pl.when(jnp.logical_and(has_left, left_local))(left.start)
        return carry

    def finish_rims(c, carry):
        wait_pieces(False, c, 0, per_parity)
        wait_pieces(False, c, per_parity, CHUNKS, jnp.logical_not(held_back))
        for step in range(1, modes):
            mode = lax.rem(me + step, modes)
            for slot in range(early):
                complete(c, mode, slot, element_of(mode, slot))
        right, left = first_copies(c)
        pl.when(jnp.logical_and(has_right, jnp.logical_not(right_local)))(right.start)
        pl.when(jnp.logical_and(has_left, jnp.logical_not(left_local)))(left.start)
        return carry

    def first_half(parity, carry):
        at = parity * per_parity
        lax.fori_loop(at, at + per_parity, first_sweep, 0)
        lax.fori_loop(at, at + per_parity, finish_rims, 0)

        @pl.when(jnp.logical_and(held_back, parity == 0))
        def _():
            wait_pieces(False, per_parity)
            if early < elems:
                start_pieces(len(spans) - 1)

        return carry

    def second_sweep(c, carry):
        for mode in range(modes):
            for slot in range(early):
                e = element_of(mode, slot)
                put_pair(rim + e, first[c, e])
        for slot in range(early, elems):
            e = element_of(me, slot)
            put_pair(rim + e, first[c, e])
        @pl.when(c == 0)
        def _():
            for side, has in enumerate((has_left, has_right)):
                half_rows = halo_first.at[side, pl.ds(0, per_parity)]
                pl.when(has)(lambda: wait_whole(half_rows, f_recv.at[side, 0]))

        pl.when(c >= per_parity)(lambda: wait_halo_recv(first_copies(c)))
        put_halo(lambda side, c, i: halo_first[side, c, i], c)
        if early < elems:
            wait_pieces(True, c)
            for step in range(1, modes):
                mode = lax.rem(me + step, modes)
                for slot in range(early, elems):
                    e = element_of(mode, slot)
                    complete(c, mode, slot, e)
                    put_pair(rim + e, first[c, e])
        applied = apply()
        shift = shifts(c)
        for e in range(group_elems):
            mode, slot = slot_of(e)
            scaling = weights[0, e] + shift * weights[1, e]
            value = first[c, e]
            part = applied[e * count : (e + 1) * count]
            start = (2 * (c % per_parity) * count + c // per_parity) * group_elems + e
            outv[pl.ds(start, count, stride=2 * group_elems), :] = value + second_weight * inverse[
                c, e
            ] * (rhs[mode, c, slot] - (part + scaling * value))
        return carry

    lax.fori_loop(0, 2, first_half, 0)
    lax.fori_loop(0, CHUNKS, second_sweep, 0)

    for side, has in enumerate((has_right, has_left)):
        pl.when(has)(lambda: wait_whole(halo_prev.at[side], p_send.at[side]))
        pl.when(has)(lambda: wait_whole(halo_first.at[side], f_send.at[side]))
    for step in range(1, modes):
        wait_whole(sent.at[step - 1], y_send.at[step - 1])


def faces_of(group_elems):
    return 3 if group_elems // 4 == 2 else 4


def body(modes, groups, velocity, previous, derivative, stiffness, coupling, reaction, axial_weight, neighbours):
    planes, elems, nodes = velocity.shape
    rows, group_elems, _ = previous.shape
    half = planes // 2
    rim = group_elems // 4
    count = rows // CHUNKS
    tables = jnp.asarray(dft_tables(planes, modes))
    run = functools.partial(kernel, modes, groups, planes, elems, group_elems, rows, nodes)
    anywhere = pl.BlockSpec(memory_space=pltpu.HBM)
    dma = pltpu.SemaphoreType.DMA
    taps = faces_of(group_elems) + 1
    scratch = [
        pltpu.VMEM((elems, planes, nodes), f32),
        pltpu.VMEM((2, group_elems, rows // 2, nodes), f32),
        pltpu.VMEM(tables.shape, bf16),
        pltpu.VMEM((nodes, nodes), f32),
        pltpu.VMEM((5, nodes, nodes), f32),
        pltpu.VMEM((2 * nodes, 2 * nodes), bf16),
        pltpu.VMEM((taps * 2 * nodes, 2 * nodes), bf16),
        pltpu.VMEM((2, 2, half, elems * nodes), bf16),
        pltpu.VMEM((modes - 1, CHUNKS, elems, count, nodes), f32),
        pltpu.VMEM((modes, CHUNKS, elems, count, nodes), f32),
        pltpu.VMEM((CHUNKS, group_elems, count, nodes), f32),
        pltpu.VMEM((CHUNKS, group_elems, count, nodes), f32),
        pltpu.VMEM((2, 2, rim, rows // 2, nodes), f32),
        pltpu.VMEM((2, CHUNKS, rim, count, nodes), f32),
        pltpu.VMEM((group_elems + 2 * rim + 1, count, 2 * nodes), bf16),
        pltpu.SMEM((2, group_elems), f32),
        pltpu.SMEM((4, group_elems), jnp.int32),
    ]
    semaphores = [
        dma((half // min(256, half),)),
        dma((min(rim, elems) + 1,)),
        dma((2 * modes - 1,)),
        dma((5,)),
        dma((modes - 1,)),
        dma((modes - 1, PIECES)),
        dma((2,)),
        dma((2, 2)),
        dma((2,)),
        dma((2, CHUNKS // 2 + 1)),
    ]
    out = pl.pallas_call(
        run,
        out_shape=pltpu.VMEM((rows * group_elems, nodes), f32),
        in_specs=[anywhere] * 9,
        out_specs=pl.BlockSpec(memory_space=pltpu.VMEM),
        scratch_shapes=scratch + semaphores,
        compiler_params=pltpu.CompilerParams(
            collective_id=0, has_side_effects=True, vmem_limit_bytes=vmem_bytes - 4 * rows * group_elems * nodes - vmem_spare
        ),
        name="advect_helmholtz",
    )(
        velocity,
        previous.reshape(rows // 2, 2, group_elems, nodes),
        tables,
        derivative,
        stiffness,
        coupling,
        reaction,
        axial_weight,
        neighbours.T,
    )
    return out.reshape(rows, group_elems, nodes)


def solution(mesh):
    return jax.shard_map(
        functools.partial(body, mesh.shape["mode"], mesh.shape["elem"]),
        mesh=mesh,
        in_specs=(
            P(None, ("elem", "mode"), None),
            P("mode", "elem", None),
            P(),
            P(),
            P(),
            P("elem"),
            P("elem"),
            P("elem", None),
        ),
        out_specs=P("mode", "elem", None),
        check_vma=False,
    )
```
